32 devices in a mesh: dp: 4 (over y, x), seq: 8 (over z, core).
Axes of the slice: x: 2, y: 2, z: 4, core: 2. Of those that a mesh axis runs over, the one named last changes fastest.
Arguments:
- tokens: bfloat16 [4, 1024, 768], P('dp', 'seq'), may hold values from -6 to 6
- lengths: int32 [4], P('dp'), may hold values from 256 to 1024, as said below
- buckets: int32 [4, 12, 1024], P('dp', None, 'seq'), may hold values from 0 to 7
- feature_proj: float32 [64, 256], replicated, may hold values from -5 to 5
- attn_gain: float32 [768], replicated, may hold values from 0.5 to 1.5
- qkv_weight: bfloat16 [768, 2304], replicated, may hold values from -0.21875 to 0.21875
- out_weight: bfloat16 [768, 768], replicated, may hold values from -0.875 to 0.875
- mlp_gain: float32 [768], replicated, may hold values from 0.5 to 1.5
- up_weight: bfloat16 [768, 3072], replicated, may hold values from -0.21875 to 0.21875
- down_weight: bfloat16 [3072, 768], replicated, may hold values from -0.109375 to 0.109375
- cotangent: bfloat16 [4, 1024, 768], P('dp', 'seq'), may hold values from -6 to 6
Outputs:
- layer_out: bfloat16 [4, 1024, 768], P('dp', 'seq')
- grad_tokens: float32 [4, 1024, 768], P('dp', 'seq')
- grad_qkv: float32 [768, 2304], P('seq')
- grad_out: float32 [768, 768], P('seq')
- grad_up: float32 [768, 3072], P('seq')
- grad_down: float32 [3072, 768], P('seq')
- grad_attn_gain: float32 [768], P('seq')
- grad_mlp_gain: float32 [768], P('seq')
The draws below stay inside these ranges and needn't reach their ends.
Inputs may be any that keep to these rules, and one draw needn't show every extreme that they name: `lengths`: positions of a row below its length hold real tokens, the rest padding; some row of every draw has the full length 1024.
All inputs are finite; a program needn't handle non-finite values.
Results may differ from the reference program's by a relative error of at most 0.012.
The reference program's roundings to bfloat16 on the way count: a program that leaves them out, or rounds other values in their place, can miss the bound.
Values may be sent and summed in bfloat16 or wider, within the bound.
No kernel may reach another device: no remote copies, remote signals or barrier semaphores. Data moves between devices by JAX's collectives and lax.ppermute only.
A program may use at most 512 MiB of HBM per device.

```python
from functools import partial
import jax
import jax.numpy as jnp
from jax import lax

D = 768
H = 12
DH = 64
FF = 3072
M = 256
SPARSE_BLOCK = 64
BUCKETS = 8
TOK_DEV = 128
ROWS = 4
LEN = 1024


def draw_lengths(key, part):
    first_key, second_key = jax.random.split(jax.random.fold_in(key, 17))
    base = jax.random.randint(first_key, (ROWS,), LEN // 4, LEN + 1)
    full_row = jax.random.randint(second_key, (), 0, ROWS)
    return jnp.where(jnp.arange(ROWS) == full_row, LEN, base).astype(jnp.int32)


def plant(array, key, low, high):
    extent = array.shape
    index_at = [jax.random.randint(jax.random.fold_in(key, axis), (), 0, extent[axis]) for axis in range(len(extent))]
    array = array.at[tuple(index_at)].set(low)
    longest = extent.index(max(extent))
    index_at[longest] = (index_at[longest] + 1) % extent[longest]
    return array.at[tuple(index_at)].set(high)


def steps_of(key, extent, cuts, low, largest):
    def one(dim, blocks):
        draws = jax.random.uniform(jax.random.fold_in(jax.random.fold_in(key, 6), dim), (blocks,), jnp.float32, low / len(cuts), largest / len(cuts))
        return jnp.repeat(jnp.exp(draws), extent[dim] // blocks).reshape((-1,) + (1,) * (len(extent) - dim - 1))

    loudness = one(*cuts[0])
    for cut in cuts[1:]:
        loudness = loudness * one(*cut)
    return loudness


def centred(key, dims, scale, bound, cuts=(), kind=jnp.bfloat16):
    values = scale * jax.random.normal(key, dims, jnp.float32)
    if cuts:
        values = values * steps_of(key, dims, cuts, -0.22, 0.18)
    return jnp.clip(values, -bound, bound).astype(kind)


def setup_inputs(seed: int = 0) -> dict:
    key_list = jax.random.split(jax.random.key(seed), 12)
    tokens = centred(key_list[0], (ROWS, LEN, D), 1.0, 6.0, ((0, 4), (1, 8)))
    lengths = draw_lengths(jax.random.fold_in(key_list[11], 71), 0)
    buckets = plant(jax.random.randint(key_list[2], (ROWS, H, LEN), 0, BUCKETS), jax.random.fold_in(key_list[2], 1), 0, BUCKETS - 1).astype(jnp.int32)
    feature_proj = centred(key_list[3], (DH, M), 1.0, 5.0, (), jnp.float32)
    attn_gain = jnp.clip(1.0 + 0.1 * jax.random.normal(key_list[4], (D,), jnp.float32), 0.5, 1.5)
    qkv_weight = centred(key_list[5], (D, 3 * D), D ** -0.5, 0.21875)
    out_weight = centred(key_list[6], (D, D), (D // 16) ** -0.5, 0.875)
    mlp_gain = jnp.clip(1.0 + 0.1 * jax.random.normal(key_list[7], (D,), jnp.float32), 0.5, 1.5)
    up_weight = centred(key_list[8], (D, FF), D ** -0.5, 0.21875)
    down_weight = centred(key_list[9], (FF, D), FF ** -0.5, 0.109375)
    cotangent = centred(key_list[10], (ROWS, LEN, D), 1.0, 6.0, ((0, 4), (1, 8)))
    return {"tokens": tokens, "lengths": lengths, "buckets": buckets, "feature_proj": feature_proj, "attn_gain": attn_gain, "qkv_weight": qkv_weight, "out_weight": out_weight, "mlp_gain": mlp_gain, "up_weight": up_weight, "down_weight": down_weight, "cotangent": cotangent}


HIGH_PRECISION = lax.Precision.HIGHEST
EPS = 1e-05

@jax.custom_vjp
def low(v):
    return lax.optimization_barrier(v.astype(jnp.bfloat16)).astype(jnp.float32)

@jax.custom_vjp
def low_back(v):
    return v

def low_keep(v):
    return (low(v), None)

def low_pass(kept, grad):
    return (grad,)

def back_keep(v):
    return (v, None)

def back_low(kept, grad):
    return (low(grad),)
low.defvjp(low_keep, low_pass)
low_back.defvjp(back_keep, back_low)

def layer_norm(value_rows, gain):
    center = value_rows - lax.optimization_barrier(jnp.mean(value_rows, -1, keepdims=True))
    spread = lax.optimization_barrier(jnp.mean(center * center, -1, keepdims=True))
    return center * lax.rsqrt(spread + EPS) * gain

def feature_map(inputs, feature_proj):
    factor = DH ** (-0.25)
    linear = jnp.einsum('lhd,dm->lhm', inputs, feature_proj, precision=HIGH_PRECISION) * factor
    square = 0.5 * factor * factor * lax.optimization_barrier(jnp.sum(inputs * inputs, -1, keepdims=True))
    return jnp.exp(linear - square) * M ** (-0.5)

def span_forward(feature_proj, row_length, carry, pieces):
    running_feature_sums, carry_norms = carry
    query, keys, value_rows, query_tags, key_tags, first_pos = pieces
    key_count = keys.shape[0]
    query_pos = first_pos + jnp.arange(TOK_DEV, dtype=jnp.int32)
    key_pos = first_pos - SPARSE_BLOCK + jnp.arange(key_count, dtype=jnp.int32)
    query_ok = query_pos < row_length
    key_ok = (key_pos >= 0) & (key_pos < row_length)
    own_flag = jnp.arange(key_count) >= SPARSE_BLOCK
    causal = key_pos[None, :] <= query_pos[:, None]
    near_block = key_pos[None, :] // SPARSE_BLOCK >= query_pos[:, None] // SPARSE_BLOCK - 1
    allowed = causal[None] & key_ok[None, None, :]
    matched = (query_tags[:, :, None] == key_tags[:, None, :]) & allowed & near_block[None]
    query_features = low(feature_map(query, feature_proj))
    feat_keys = low(feature_map(keys, feature_proj))
    scores = jnp.einsum('thd,jhd->htj', query, keys, precision=HIGH_PRECISION) * DH ** (-0.5)
    exponent = jnp.exp(scores)
    approx = jnp.einsum('thm,jhm->htj', query_features, feat_keys, precision=HIGH_PRECISION)
    blended = jnp.where(matched, jnp.where(own_flag, exponent, exponent - approx), jnp.where(own_flag & allowed, approx, 0.0))
    blended_low = low(blended)
    attention_numerator = jnp.einsum('enb,nbs->ens', query_features, running_feature_sums, precision=HIGH_PRECISION)
    attention_numerator = attention_numerator + jnp.einsum('htj,jhd->thd', blended_low, value_rows, precision=HIGH_PRECISION)
    denominator = jnp.einsum('thm,hm->th', query_features, carry_norms, precision=HIGH_PRECISION) + lax.optimization_barrier(jnp.sum(blended, -1)).T
    den_safe = jnp.where(query_ok[:, None], denominator, 1.0)
    attended = jnp.where(query_ok[:, None, None], attention_numerator / den_safe[:, :, None], 0.0)
    retained_features = feat_keys[SPARSE_BLOCK:] * key_ok[SPARSE_BLOCK:, None, None].astype(jnp.float32)
    updated_sums = running_feature_sums + jnp.einsum('wau,waj->auj', retained_features, value_rows[SPARSE_BLOCK:], precision=HIGH_PRECISION)
    new_norms = carry_norms + lax.optimization_barrier(jnp.sum(retained_features, 0))
    return ((updated_sums, new_norms), attended)

def row_attention(query, keys, value_rows, row_buckets, row_length, feature_proj):
    steps = LEN // TOK_DEV
    key_pad = jnp.concatenate([jnp.zeros((SPARSE_BLOCK, H, DH), jnp.float32), keys], 0)
    value_pad = jnp.concatenate([jnp.zeros((SPARSE_BLOCK, H, DH), jnp.float32), value_rows], 0)
    tag_pad = jnp.concatenate([jnp.zeros((H, SPARSE_BLOCK), jnp.int32), row_buckets], 1)
    starts = jnp.arange(steps, dtype=jnp.int32) * TOK_DEV
    key_win = jax.vmap(lambda begin: lax.dynamic_slice_in_dim(key_pad, begin, TOK_DEV + SPARSE_BLOCK, 0))(starts)
    value_win = jax.vmap(lambda begin: lax.dynamic_slice_in_dim(value_pad, begin, TOK_DEV + SPARSE_BLOCK, 0))(starts)
    tag_win = jax.vmap(lambda begin: lax.dynamic_slice_in_dim(tag_pad, begin, TOK_DEV + SPARSE_BLOCK, 1))(starts)
    query_spans = query.reshape(steps, TOK_DEV, H, DH)
    query_tags = row_buckets.reshape(H, steps, TOK_DEV).transpose(1, 0, 2)
    start_carry = (jnp.zeros((H, M, DH), jnp.float32), jnp.zeros((H, M), jnp.float32))
    stepper = jax.checkpoint(partial(span_forward, feature_proj, row_length))
    final_carry, attended = lax.scan(stepper, start_carry, (query_spans, key_win, value_win, query_tags, tag_win, starts))
    return attended.reshape(LEN, H * DH)

def row_forward(row_in, row_buckets, row_length, feature_proj, attn_gain, qkv_weight, out_weight, mlp_gain, up_weight, down_weight):
    normed_in = low(layer_norm(row_in, attn_gain))
    qkv = low_back(low(jnp.dot(normed_in, qkv_weight, precision=HIGH_PRECISION)))
    query = qkv[:, :D].reshape(LEN, H, DH)
    keys = qkv[:, D:2 * D].reshape(LEN, H, DH)
    value_rows = qkv[:, 2 * D:].reshape(LEN, H, DH)
    attended = row_attention(query, keys, value_rows, row_buckets, row_length, feature_proj)
    attended = low_back(low(attended))
    mid_resid = row_in + jnp.dot(attended, out_weight, precision=HIGH_PRECISION)
    normed_mid = low(layer_norm(mid_resid, mlp_gain))
    pre_act = low_back(jnp.dot(normed_mid, up_weight, precision=HIGH_PRECISION))
    hidden = low(jax.nn.gelu(pre_act, approximate=True))
    return mid_resid + jnp.dot(hidden, down_weight, precision=HIGH_PRECISION)

def reference(tokens, lengths, buckets, feature_proj, attn_gain, qkv_weight, out_weight, mlp_gain, up_weight, down_weight, cotangent):
    params = (attn_gain, qkv_weight.astype(jnp.float32), out_weight.astype(jnp.float32), mlp_gain, up_weight.astype(jnp.float32), down_weight.astype(jnp.float32))
    zeros = tuple((jnp.zeros_like(param) for param in params))

    def per_row(totals, pieces):
        row_tokens, row_buckets, row_length, row_cot = pieces

        def forward(row_in, *weights):
            return row_forward(row_in, row_buckets, row_length, feature_proj, *weights)
        row_out, pullback = jax.vjp(forward, row_tokens.astype(jnp.float32), *params)
        gradients = pullback(row_cot.astype(jnp.float32))
        totals = tuple((total + grad for total, grad in zip(totals, gradients[1:])))
        return (totals, (row_out.astype(jnp.bfloat16), gradients[0]))
    totals, (layer_outs, grad_in) = lax.scan(per_row, zeros, (tokens, buckets, lengths, cotangent))
    return (layer_outs, grad_in, totals[1], totals[2], totals[4], totals[5], totals[0], totals[3])
```

```python
import functools

import jax
import jax.numpy as jnp
from jax import lax
from jax.experimental import pallas as pl
from jax.experimental.pallas import tpu as pltpu
from jax.sharding import PartitionSpec as P

EPS = 1e-05
F32 = jnp.float32
BF = jnp.bfloat16
T = 128
D = 768
H = 12
HD = 64
M = 256
HM = H * M
PAIRS = H // 2
EDGE = 64
WIN = 640
ROWS_1 = 120
ROWS_2 = 96
ROWS_B = 104
MIB = 1 << 20


def nn(a, b):
    return lax.dot_general(a, b, (((1,), (0,)), ((), ())), preferred_element_type=F32)


def nt(a, b):
    return lax.dot_general(a, b, (((1,), (1,)), ((), ())), preferred_element_type=F32)


def tn(a, b):
    return lax.dot_general(a, b, (((0,), (0,)), ((), ())), preferred_element_type=F32)


def split(a):
    high = a.astype(BF)
    return high, (a - high.astype(F32)).astype(BF)


def iota(shape, axis):
    return lax.broadcasted_iota(jnp.int32, shape, axis)


def lanes(*parts):
    return jnp.concatenate(parts, axis=1)


def norm_parts(value):
    center = value - jnp.mean(value, -1, keepdims=True)
    scale = lax.rsqrt(jnp.mean(center * center, -1, keepdims=True) + EPS)
    return center * scale, scale


def norm_back(unit, scale, gain, upstream):
    inner = upstream * gain
    return scale * (
        inner
        - jnp.mean(inner, -1, keepdims=True)
        - unit * jnp.mean(inner * unit, -1, keepdims=True)
    )


def phi_pair(pair, proj):
    linear = nn(lanes(pair, pair), proj)
    wide = pair.astype(F32)
    square = wide * wide
    first = iota(square.shape, 1) < HD
    out = []
    for half in range(2):
        mine = first if half == 0 else ~first
        total = jnp.sum(jnp.where(mine, square, 0.0), -1, keepdims=True)
        out.append(
            jnp.exp(linear[:, half * M : half * M + M] - total * (0.5 * HD**-0.5)) * M**-0.5
        )
    return out


def phi_back(pair, grads, phis, proj):
    weighted = [grad * phi for grad, phi in zip(grads, phis)]
    joined = lanes(*weighted)
    high, low = split(joined)
    linear = nt(high, proj[:128]) + nt(high, proj[128:]) + nt(low, proj[:128])
    sums = [jnp.sum(part, -1, keepdims=True) for part in weighted]
    first = iota(pair.shape, 1) < HD
    return linear - HD**-0.5 * pair.astype(F32) * jnp.where(first, sums[0], sums[1])


def pick(first, two):
    return jnp.where(first, two[0], two[1])


def masked(first, half, value):
    zero = jnp.zeros_like(value)
    return jnp.where(first, value, zero) if half == 0 else jnp.where(first, zero, value)


def columns_to(acc, head, column):
    return jnp.where(iota(acc.shape, 1) == head, column, acc)


def rounded(value):
    return value.astype(BF)


def call(kernel, scalars, args, in_specs, outs, out_specs, grid, scratch=(), flops=0, size=0, vmem=48, aliases=None):
    return pl.pallas_call(
        kernel,
        out_shape=outs,
        grid_spec=pltpu.PrefetchScalarGridSpec(
            num_scalar_prefetch=1,
            grid=grid,
            in_specs=in_specs,
            out_specs=out_specs,
            scratch_shapes=list(scratch),
        ),
        input_output_aliases=aliases or {},
        compiler_params=pltpu.CompilerParams(vmem_limit_bytes=vmem * MIB),
        cost_estimate=pl.CostEstimate(flops=flops // 1000, bytes_accessed=size // 1000, transcendentals=0),
    )(scalars, *args)


def whole(shape):
    return pl.BlockSpec(memory_space=pltpu.VMEM)


def sds(shape, dtype):
    return jax.ShapeDtypeStruct(shape, dtype)


def projection(feature_proj):
    scaled = feature_proj * HD ** (-0.25)
    high, low = split(scaled)
    none = jnp.zeros((HD, M), BF)
    return jnp.concatenate([lanes(high, none), lanes(none, high), lanes(low, none), lanes(none, low)], 0)


def own_kernel(
    sc, x_ref, gain_ref, w_ref, feature_ref, g_ref, tag_ref,
    pay_ref, qkv_ref, phiq_ref, phik_ref, expo_ref, blend_ref, num_ref, den_ref, proj_ref, tags_ref,
):
    unit, _ = norm_parts(x_ref[...].astype(F32))
    normed = unit * gain_ref[...]
    low = normed.astype(BF)
    pay_ref[0:D, :] = normed.T.astype(BF)
    for t in range(6):
        pay_ref[D + 128 * t : D + 128 * t + 128, :] = g_ref[:, 128 * t : 128 * t + 128]
    qkv_ref[...] = nn(low, w_ref[...]).astype(BF)
    rows = jnp.concatenate([tag_ref[...].astype(F32), jnp.zeros((4, T), F32)], 0)
    tags_ref[...] = rows.astype(BF)
    cols = rows.T
    first = iota((T, 128), 1) < HD
    query_at, key_at = iota((T, T), 0), iota((T, T), 1)
    allowed = (key_at <= query_at) & (key_at + sc[0] * T < sc[1])
    dens = jnp.zeros((T, 128), F32)
    proj = projection(feature_ref[...])
    proj_ref[...] = proj
    for p in range(PAIRS):
        at = slice(128 * p, 128 * p + 128)
        query, key, value = (
            qkv_ref[:, part * D + 128 * p : part * D + 128 * p + 128] for part in range(3)
        )
        phi_q, phi_k = phi_pair(query, proj), phi_pair(key, proj)
        nums = []
        for half in range(2):
            h = 2 * p + half
            phiq_ref[:, M * h : M * h + M] = phi_q[half]
            phik_ref[:, M * h : M * h + M] = phi_k[half]
            expo = jnp.exp(nt(masked(first, half, query), key) * HD**-0.5)
            approx = nt(phi_q[half].astype(BF), phi_k[half].astype(BF))
            matched = allowed & (cols[:, h : h + 1] == rows[h : h + 1, :])
            blend = jnp.where(matched, expo, jnp.where(allowed, approx, 0.0))
            expo_ref[h] = jnp.where(matched, expo, 0.0)
            blend_ref[h] = blend.astype(BF)
            nums.append(nn(blend.astype(BF), value))
            dens = columns_to(dens, h, jnp.sum(blend, -1, keepdims=True))
        num_ref[:, at] = pick(first, nums)
    den_ref[...] = dens


def own_forward(scalars, own, gain, qkv_weight, feature_proj, cotangent, tags):
    outs = (
        sds((2 * D, 128), BF), sds((T, 3 * D), BF), sds((T, HM), F32), sds((T, HM), F32),
        sds((H, T, T), F32), sds((H, T, T), BF), sds((T, D), F32), sds((T, 128), F32),
        sds((2 * 128, 2 * M), BF), sds((16, T), BF),
    )
    args = (own, gain, qkv_weight, feature_proj, cotangent, tags)
    return call(
        own_kernel, scalars, args, [whole(a.shape) for a in args], outs,
        [whole(o.shape) for o in outs], (1,), vmem=6, flops=2_000_000_000, size=9_000_000,
    )


def others_kernel(begin, sc, x_ref, gain_ref, w_ref, proj_ref, *refs):
    u_ref, v_ref, phi_ref, sums_ref, norms_ref = refs[-5:]
    slot = pl.program_id(0)
    span = sc[8 + begin + slot]

    @pl.when(slot == 0)
    def _():
        if begin:
            sums_ref[...], norms_ref[...] = refs[3][...], refs[4][...]
        else:
            sums_ref[...] = jnp.zeros_like(sums_ref)
            norms_ref[...] = jnp.zeros_like(norms_ref)

    unit, _ = norm_parts(x_ref[0].astype(F32))
    low = (unit * gain_ref[...]).astype(BF)
    earlier = span < sc[0]
    offset = pl.multiple_of(jnp.where(earlier, D, 0), D)
    u_ref[0] = nn(low, w_ref[:, pl.ds(offset, D)]).astype(BF)
    proj = proj_ref[...]
    for p in range(PAIRS):
        phis = phi_pair(u_ref[0, :, 128 * p : 128 * p + 128], proj)
        for half in range(2):
            h = 2 * p + half
            phi_ref[0, :, M * h : M * h + M] = phis[half].astype(BF)

    @pl.when(earlier)
    def _():
        value = nn(low, w_ref[:, 2 * D : 3 * D])
        v_ref[0] = value.astype(BF)
        valid = iota((D, T), 1) + span * T < sc[1]
        turned = jnp.where(valid, value.T, 0.0).astype(BF)
        for h in range(H):
            sums_ref[HD * h : HD * h + HD, :] += nn(
                turned[HD * h : HD * h + HD, :], phi_ref[0, :, M * h : M * h + M]
            )
        ones = jnp.where(iota((8, T), 1) + span * T < sc[1], 1.0, 0.0).astype(BF)
        norms_ref[...] += nn(ones, phi_ref[0])

    @pl.when(~earlier)
    def _():
        v_ref[0] = jnp.zeros((T, D), BF)


def others_forward(scalars, begin, pieces, gain, qkv_weight, proj, so_far=()):
    count, spans = pieces.shape[0], 7
    outs = (
        sds((spans, T, D), BF), sds((spans, T, D), BF), sds((spans, T, HM), BF),
        sds((D, M), F32), sds((8, HM), F32),
    )
    step = lambda i, sc: (begin + i, 0, 0)
    specs = [pl.BlockSpec((1, T, D), lambda i, sc: (i, 0, 0))]
    specs += [whole(a.shape) for a in (gain, qkv_weight, proj)]
    aliases = {}
    if so_far:
        specs += [pl.BlockSpec(memory_space=pl.ANY)] * 3 + [whole(a.shape) for a in so_far[3:]]
        aliases = {5: 0, 6: 1, 7: 2}
    return call(
        functools.partial(others_kernel, begin), scalars, (pieces, gain, qkv_weight, proj, *so_far), specs,
        outs,
        [pl.BlockSpec((1, T, D), step), pl.BlockSpec((1, T, D), step), pl.BlockSpec((1, T, HM), step),
         whole((D, M)), whole((8, HM))],
        (count,), vmem=8, flops=count * 600_000_000, size=count * 1_400_000 + 3_500_000, aliases=aliases,
    )


def own_cols(tags_ref):
    return tags_ref[...].astype(F32).T.astype(BF)


def middle_kernel(
    sc, x_ref, qkv_ref, phiq_ref, sums_ref, norms_ref, numl_ref, denl_ref, tags_ref, tags_prev,
    up_prev, vp_prev, phi_prev, gain_ref, wo_ref, wup_ref, wdown_ref, g_ref,
    a0, a1, a2, a3, b0, b1, b2, b3, out_ref, dmid_ref, dn_low_ref, dn_ref, dd_ref, expo_ref, blend_ref, gain_out,
    mid_s, nm_s, acc_s, dnm_s, num_s, den_s, turn_s,
):
    first_pay, second_pay = (a0, a1, a2, a3), (b0, b1, b2, b3)
    step = pl.program_id(0)
    me = sc[6]
    first = iota((T, 128), 1) < HD
    valid = iota((T, 1), 0) + sc[0] * T < sc[1]

    @pl.when(step == 0)
    def _():
        own = tags_ref[...].astype(F32).T
        prev = tags_prev[...].astype(F32)
        prev_tag = [prev[h : h + 1, EDGE:T] for h in range(H)]
        edge_first = iota((EDGE, 128), 1) < HD
        edge_ok = (sc[4] > 0) & (iota((EDGE, EDGE), 1) + (sc[0] * T - EDGE) < sc[1])
        dens = denl_ref[...]
        zeros = jnp.zeros((EDGE, 128), F32)
        for p in range(PAIRS):
            at = slice(128 * p, 128 * p + 128)
            high, lowp = split(sums_ref[at, :])
            query = qkv_ref[0:EDGE, at]
            key, value = up_prev[0, :, at], vp_prev[0, :, at]
            nums = []
            for half in range(2):
                h = 2 * p + half
                hm = slice(M * h, M * h + M)
                phi_q = phiq_ref[:, hm].astype(BF)
                total = nt(phi_q, high) + nt(phi_q, lowp)
                den = jnp.sum(phi_q.astype(F32) * norms_ref[0:1, hm], -1, keepdims=True)
                expo = jnp.exp(nt(masked(edge_first, half, query), key) * HD**-0.5)
                approx = nt(phi_q[0:EDGE], phi_prev[0, :, hm])
                matched = edge_ok & (own[0:EDGE, h : h + 1] == prev_tag[h])
                blend = jnp.where(matched, expo - approx, 0.0)
                expo_ref[h] = jnp.where(matched, expo, 0.0)
                blend_ref[h] = blend.astype(BF)
                total = total + jnp.concatenate([nn(blend.astype(BF), value), zeros], 0)
                den = den + jnp.concatenate(
                    [jnp.sum(blend, -1, keepdims=True), jnp.zeros((EDGE, 1), F32)], 0
                )
                nums.append(total)
                dens = jnp.where(iota(dens.shape, 1) == h, dens + den, dens)
            num_s[:, at] = numl_ref[:, at] + pick(first, nums)
        dens = jnp.where(valid, dens, 1.0)
        den_s[...] = dens
        for p in range(PAIRS):
            at = slice(128 * p, 128 * p + 128)
            den = jnp.where(first, dens[:, 2 * p : 2 * p + 1], dens[:, 2 * p + 1 : 2 * p + 2])
            mid_s[:, at] = jnp.where(valid, num_s[:, at] / den, 0.0)
        attended = mid_s[...].astype(BF)
        turned = mid_s[...].T.astype(BF)
        for k in range(4):
            upper = (me ^ k) >= 2
            for s in range(8):
                first_pay[k][768 + 48 * s : 768 + 48 * s + 48, :] = jnp.where(
                    upper, turned[96 * s + 48 : 96 * s + 96, :], turned[96 * s : 96 * s + 48, :]
                )
        mid = x_ref[...].astype(F32) + nn(attended, wo_ref[...])
        mid_s[...] = mid
        unit, _ = norm_parts(mid)
        normed = unit * gain_ref[...]
        nm_s[...] = normed.astype(BF)
        turned = normed.T.astype(BF)
        for k in range(4):
            second_pay[k][0:D, :] = turned
        acc_s[...] = jnp.zeros_like(acc_s)
        dnm_s[...] = jnp.zeros_like(dnm_s)

    pre = nn(nm_s[...], wup_ref[...])
    grad_hidden = nt(g_ref[...], wdown_ref[...])
    root = (2.0 / jnp.pi) ** 0.5
    inner = root * (pre + 0.044715 * (pre * pre * pre))
    tanh = jnp.tanh(inner)
    half_up = 0.5 * (1.0 + tanh)
    hidden = pre * half_up
    slope = half_up + 0.5 * pre * (1.0 - tanh * tanh) * (root * (1.0 + 3 * 0.044715 * (pre * pre)))
    grad_pre = (grad_hidden * slope).astype(BF)
    hidden_low = hidden.astype(BF)
    acc_s[...] += nn(hidden_low, wdown_ref[...])
    dnm_s[...] += nt(grad_pre, wup_ref[...])
    turn_s[...] = hidden.T.astype(BF)
    for k in range(4):
        for s in range(2):
            base = pl.multiple_of(192 * step + 96 * s, 96)
            begin = pl.multiple_of(384 * s + 96 * (k ^ me), 96)
            first_pay[k][pl.ds(base, 96), :] = turn_s[pl.ds(begin, 96), :]

        @pl.when((step ^ me) == k)
        def _():
            for t in range(6):
                second_pay[k][D + 128 * t : D + 128 * t + 128, :] = grad_pre[:, 128 * t : 128 * t + 128]

    @pl.when(step == 3)
    def _():
        mid = mid_s[...]
        out_ref[...] = (mid + acc_s[...]).astype(BF)
        unit, scale = norm_parts(mid)
        grad = dnm_s[...]
        gain_out[...] = jnp.broadcast_to(jnp.sum(grad * unit, 0, keepdims=True), (8, D))
        dmid = g_ref[...].astype(F32) + norm_back(unit, scale, gain_ref[...], grad)
        dmid_ref[...] = dmid
        high, low = split(dmid)
        for k in range(4):
            right = ((me ^ k) & 1) > 0
            for t in range(3):
                first_pay[k][1152 + 128 * t : 1152 + 128 * t + 128, :] = jnp.where(
                    right, high[:, 384 + 128 * t : 512 + 128 * t], high[:, 128 * t : 128 * t + 128]
                )
        datt = (nt(high, wo_ref[...]) + nt(low, wo_ref[...])).astype(BF).astype(F32)
        dens = den_s[...]
        ddens = jnp.zeros((T, 128), F32)
        for p in range(PAIRS):
            at = slice(128 * p, 128 * p + 128)
            den = jnp.where(first, dens[:, 2 * p : 2 * p + 1], dens[:, 2 * p + 1 : 2 * p + 2])
            dnum = jnp.where(valid, datt[:, at] / den, 0.0)
            dn_ref[:, at] = dnum
            dn_low_ref[:, at] = dnum.astype(BF)
            prod = dnum * num_s[:, at]
            for half in range(2):
                h = 2 * p + half
                total = jnp.sum(masked(first, half, prod), -1, keepdims=True)
                ddens = columns_to(ddens, h, -total / dens[:, h : h + 1])
        dd_ref[...] = ddens
        dn_low_ref[:, D : D + 16] = ddens[:, 0:16].astype(BF)
        dn_low_ref[:, D + 16 : D + 32] = own_cols(tags_ref)
        dn_low_ref[:, D + 32 : D + 128] = jnp.zeros((T, 96), BF)


def middle(scalars, own, qkv, phi_q, sums, norms, num, den, tags, tags_prev, others, gain, wo, wup, wdown, cot):
    u, v, phi = others
    prev = lambda i, sc: (sc[2], 1, 0)
    outs = tuple([sds((2 * D, 128), BF)] * 8) + (
        sds((T, D), BF), sds((T, D), F32), sds((T, D + 128), BF),
        sds((T, D), F32), sds((T, 128), F32), sds((H, EDGE, EDGE), F32), sds((H, EDGE, EDGE), BF),
        sds((8, D), F32),
    )
    args = (own, qkv, phi_q, sums, norms, num, den, tags, tags_prev, u, v, phi, gain, wo, wup, wdown, cot)
    specs = [whole(a.shape) for a in args[:9]] + [
        pl.BlockSpec((1, EDGE, D), prev), pl.BlockSpec((1, EDGE, D), prev),
        pl.BlockSpec((1, EDGE, HM), prev),
        whole(gain.shape), whole(wo.shape),
        pl.BlockSpec((D, D), lambda i, sc: (0, i)), pl.BlockSpec((D, D), lambda i, sc: (i, 0)),
        whole(cot.shape),
    ]
    scratch = [
        pltpu.VMEM((T, D), F32), pltpu.VMEM((T, D), BF), pltpu.VMEM((T, D), F32),
        pltpu.VMEM((T, D), F32), pltpu.VMEM((T, D), F32), pltpu.VMEM((T, 128), F32),
        pltpu.VMEM((D, T), BF),
    ]
    return call(
        middle_kernel, scalars, args, specs, outs, [whole(o.shape) for o in outs], (4,), scratch,
        vmem=12, flops=3_500_000_000, size=20_000_000,
    )


def own_back_kernel(
    sc, tags_ref, tags_prev, qkv_ref, phiq_ref, phik_ref, proj_ref, expo_ref, blend_ref, dn_ref, dd_ref,
    sums_ref, norms_ref, up_prev, vp_prev, phi_prev, expo_e, blend_e,
    dq_ref, dk_ref, dv_ref, dphi_ref,
):
    rows = tags_ref[...].astype(F32)
    cols = rows.T
    first = iota((T, 128), 1) < HD
    query_at, key_at = iota((T, T), 0), iota((T, T), 1)
    allowed = (key_at <= query_at) & (key_at + sc[0] * T < sc[1])
    prev_tag = tags_prev[...].astype(F32)
    edge_first = iota((EDGE, 128), 1) < HD
    edge_ok = (sc[4] > 0) & (iota((EDGE, EDGE), 1) + (sc[0] * T - EDGE) < sc[1])
    proj = proj_ref[...]
    for p in range(PAIRS):
        at = slice(128 * p, 128 * p + 128)
        query, key, value = (
            qkv_ref[:, part * D + 128 * p : part * D + 128 * p + 128] for part in range(3)
        )
        key_e, value_e = up_prev[0, :, at], vp_prev[0, :, at]
        high, low = split(dn_ref[:, at])
        both = lanes(high, low)
        s_high, s_low = split(sums_ref[at, :])
        grads, phis, dqs, dks, dvs = [], [], [], [], []
        for half in range(2):
            h = 2 * p + half
            hm = slice(M * h, M * h + M)
            dden = dd_ref[:, h : h + 1]
            mine = lanes(masked(first, half, high), masked(first, half, low))
            phi_q, phi_k = phiq_ref[:, hm], phik_ref[:, hm]
            dw = nt(mine, lanes(value, value)) + dden
            matched = cols[:, h : h + 1] == rows[h : h + 1, :]
            ds = (dw * expo_ref[h] * HD**-0.5).astype(BF)
            da = jnp.where(allowed & ~matched, dw, 0.0).astype(BF)
            dq = nn(ds, key)
            dks.append(tn(ds, query))
            dv = tn(blend_ref[h], both)
            dvs.append(dv[:, 0:128] + dv[:, 128:256])
            dphi = nn(da, phi_k.astype(BF)) + dden * norms_ref[0:1, hm]
            dphi = dphi + nn(mine, jnp.concatenate([s_high, s_high], 0))
            dphi = dphi + nn(mine[:, 0:128], s_low)
            dphi_ref[:, hm] = tn(da, phi_q.astype(BF))
            edge = nt(mine[0:EDGE], lanes(value_e, value_e)) + dden[0:EDGE]
            matched_e = edge_ok & (cols[0:EDGE, h : h + 1] == prev_tag[h : h + 1, EDGE:T])
            ds_e = (edge * expo_e[h] * HD**-0.5).astype(BF)
            da_e = jnp.where(matched_e, -edge, 0.0).astype(BF)
            dqs.append(dq + jnp.concatenate([nn(ds_e, key_e), jnp.zeros((EDGE, 128), F32)], 0))
            grads.append(
                dphi + jnp.concatenate([nn(da_e, phi_prev[0, :, hm]), jnp.zeros((EDGE, M), F32)], 0)
            )
            phis.append(phi_q)
        dq_ref[:, at] = (pick(first, dqs) + phi_back(query, grads, phis, proj)).astype(BF)
        dk_ref[:, at] = pick(first, dks)
        dv_ref[:, at] = pick(first, dvs)


def own_back(scalars, tags, tags_prev, qkv, phi_q, phi_k, proj, expo, blend, dnum, dden, sums, norms, others, expo_e, blend_e):
    u, v, phi = others
    prev = lambda i, sc: (sc[2], 1, 0)
    args = (
        tags, tags_prev, qkv, phi_q, phi_k, proj, expo, blend, dnum, dden, sums, norms, u, v, phi, expo_e,
        blend_e,
    )
    specs = [whole(a.shape) for a in args[:12]] + [
        pl.BlockSpec((1, EDGE, D), prev), pl.BlockSpec((1, EDGE, D), prev),
        pl.BlockSpec((1, EDGE, HM), prev),
        whole(expo_e.shape), whole(blend_e.shape),
    ]
    outs = (sds((T, D), BF), sds((T, D), F32), sds((T, D), F32), sds((T, HM), F32))
    return call(
        own_back_kernel, scalars, args, specs, outs, [whole(o.shape) for o in outs], (1,),
        vmem=8, flops=3_000_000_000, size=9_000_000,
    )


def last_kernel(
    sc, dn_slot, phi_slot, x_ref, tags_ref, qkv_ref, phik_ref, proj_ref, dq_ref, dk_ref, dv_ref, dphi_ref,
    u_next, phi_next, dn_next, dmid_ref, gain_ref, w_ref, gmlp_ref,
    a0, a1, a2, a3, grad_ref, sums_s, norms_s, dqkv_s,
):
    slot = pl.program_id(0)
    span = sc[24 + slot]

    @pl.when(slot == 0)
    def _():
        sums_s[...] = jnp.zeros_like(sums_s)
        norms_s[...] = jnp.zeros_like(norms_s)

    @pl.when(span > sc[0])
    def _():
        turned = dn_slot[0].astype(F32).T.astype(BF)
        for h in range(H):
            hm = slice(M * h, M * h + M)
            sums_s[HD * h : HD * h + HD, :] += nn(turned[HD * h : HD * h + HD, :], phi_slot[0, :, hm])
        norms_s[...] += nn(turned[D : D + 16, :], phi_slot[0])

    @pl.when(slot == pl.num_programs(0) - 1)
    def _():
        me = sc[6]
        rows = tags_ref[...].astype(F32)
        next_cols = dn_next[0, :, D + 16 : D + 32].astype(F32)
        first = iota((T, 128), 1) < HD
        edge_first = iota((EDGE, 128), 1) < HD
        valid = iota((T, 1), 0) + sc[0] * T < sc[1]
        edge_ok = (sc[5] > 0) & (iota((EDGE, EDGE), 1) + (sc[0] * T + EDGE) < sc[1])
        proj = proj_ref[...]
        ddn = dn_next[0, :, D : D + 128].astype(F32)
        dqkv_s[:, 0:D] = dq_ref[...]
        for p in range(PAIRS):
            at = slice(128 * p, 128 * p + 128)
            key, value = (qkv_ref[:, part * D + 128 * p : part * D + 128 * p + 128] for part in (1, 2))
            high, low = split(sums_s[at, :])
            query_n, dnum_n = u_next[0, :, at], dn_next[0, :, at]
            grads, phis, dks, dvs = [], [], [], []
            for half in range(2):
                h = 2 * p + half
                hm = slice(M * h, M * h + M)
                phi_k = phik_ref[:, hm]
                phi_kb = phi_k.astype(BF)
                mine = masked(first, half, value)
                carry = nn(mine, high) + nn(mine, low) + norms_s[h : h + 1, hm]
                dv = nt(phi_kb, high) + nt(phi_kb, low)
                q_h, d_h = masked(edge_first, half, query_n), masked(edge_first, half, dnum_n)
                phi_n = phi_next[0, :, hm]
                expo = jnp.exp(nt(q_h, key[EDGE:]) * HD**-0.5)
                approx = nt(phi_n, phi_kb[EDGE:])
                matched = edge_ok & (next_cols[0:EDGE, h : h + 1] == rows[h : h + 1, EDGE:128])
                blend = jnp.where(matched, expo - approx, 0.0).astype(BF)
                dw = nt(d_h, value[EDGE:]) + ddn[:, h : h + 1]
                ds = jnp.where(matched, dw * expo * HD**-0.5, 0.0).astype(BF)
                da = jnp.where(matched, -dw, 0.0).astype(BF)
                none = jnp.zeros((EDGE, 128), F32)
                dks.append(jnp.concatenate([none, tn(ds, query_n)], 0))
                dvs.append(jnp.where(valid, dv, 0.0) + jnp.concatenate([none, tn(blend, dnum_n)], 0))
                grads.append(
                    dphi_ref[:, hm] + jnp.where(valid, carry, 0.0)
                    + jnp.concatenate([jnp.zeros((EDGE, M), F32), tn(da, phi_n)], 0)
                )
                phis.append(phi_k)
            dqkv_s[:, D + 128 * p : D + 128 * p + 128] = (
                dk_ref[:, at] + pick(first, dks) + phi_back(key, grads, phis, proj)
            ).astype(BF)
            dqkv_s[:, 2 * D + 128 * p : 2 * D + 128 * p + 128] = (dv_ref[:, at] + pick(first, dvs)).astype(BF)
        grad = nt(dqkv_s[...], w_ref[...])
        unit, scale = norm_parts(x_ref[...].astype(F32))
        grad_ref[...] = dmid_ref[...] + norm_back(unit, scale, gain_ref[...], grad)
        attn = jnp.sum(grad * unit, 0, keepdims=True)
        mlp = gmlp_ref[0:1, :]
        row = iota((8, WIN), 0)
        gains = jnp.zeros((8, WIN), F32)
        tail = jnp.zeros((1, 2 * WIN - D), F32)
        for at, part in enumerate((attn, mlp)):
            gains = jnp.where(row == 2 * at, part[:, 0:WIN], gains)
            gains = jnp.where(row == 2 * at + 1, lanes(part[:, WIN:D], tail), gains)
        for k, pay_ref in enumerate((a0, a1, a2, a3)):
            mate = me ^ k
            begin = pl.multiple_of(jnp.where(mate == 0, 0, 128 * (4 * mate + 1)), 128)
            pay_ref[0:T, :] = dqkv_s[:, pl.ds(begin, WIN)]
            pay_ref[T : T + 8, :] = gains.astype(BF)


def last(scalars, dn_pieces, others, own, tags, qkv, phi_k, proj, dq, dk, dv, dphi, dmid, gain, qkv_weight, gmlp):
    u, v, phi = others
    count = dn_pieces.shape[0] - 1
    follow = lambda i, sc: (sc[3], 0, 0)
    args = (
        dn_pieces, phi, own, tags, qkv, phi_k, proj, dq, dk, dv, dphi, u, phi, dn_pieces, dmid, gain,
        qkv_weight, gmlp,
    )
    specs = [
        pl.BlockSpec((1, T, D + 128), lambda i, sc: (i + 1, 0, 0)),
        pl.BlockSpec((1, T, HM), lambda i, sc: (sc[40 + i], 0, 0)),
    ]
    specs += [whole(a.shape) for a in args[2:11]]
    specs += [
        pl.BlockSpec((1, EDGE, D), follow), pl.BlockSpec((1, EDGE, HM), follow),
        pl.BlockSpec((1, EDGE, D + 128), lambda i, sc: (sc[7], 0, 0)),
    ] + [whole(a.shape) for a in args[14:]]
    outs = tuple([sds((T + 8, WIN), BF)] * 4) + (sds((T, D), F32),)
    return call(
        last_kernel, scalars, args, specs, outs, [whole(o.shape) for o in outs], (count,),
        [pltpu.VMEM((D, M), F32), pltpu.VMEM((16, HM), F32), pltpu.VMEM((T, 3 * D), BF)],
        vmem=10, flops=3_000_000_000, size=count * 1_000_000 + 10_000_000,
    )


def reverse3(at):
    return ((at & 1) << 2) | (at & 2) | (at >> 2)


def place(sc, chunk_of, keep_ref, send_ref):
    for r in range(8):
        block = reverse3(r) ^ sc[0]
        target = keep_ref.at[r] if r < 4 else send_ref.at[r - 4]
        chunk_of(block, target)


def joined(parts, begin, size):
    return lanes(*[part[begin : begin + size, :] for part in parts])


def tiles(part, begin, count):
    return lanes(*[part[begin + 128 * t : begin + 128 * t + 128, :] for t in range(count)])


def product(lefts, rights):
    first = nn(lanes(lefts[0], lefts[1]), jnp.concatenate(rights[0:2], 0))
    return first + nn(lanes(lefts[2], lefts[3]), jnp.concatenate(rights[2:4], 0))


def first_kernel(sc, p0, p1, p2, p3, e0, e1, e2, e3, keep_ref, send_ref, down_s, out_s):
    parts = (p0, p1, p2, p3)
    cots = [e[D : 2 * D, :] for e in (e0, e1, e2, e3)]
    down_s[...] = product([a[0:768, :] for a in parts], [tiles(a, 0, 6) for a in cots])
    out_s[...] = product([a[768:1152, :] for a in parts], [tiles(a, 1152, 3) for a in parts])

    def chunk(block, target):
        at = pl.multiple_of(96 * block, 96)
        target[0:96, :] = down_s[pl.ds(at, 96), :].astype(target.dtype)
        at = pl.multiple_of(48 * block, 48)
        target[96:120, 0:384] = out_s[pl.ds(at, 24), :].astype(target.dtype)
        at = pl.multiple_of(48 * block + 24, 24)
        target[96:120, 384:768] = out_s[pl.ds(at, 24), :].astype(target.dtype)

    place(sc, chunk, keep_ref, send_ref)


def second_kernel(sc, p0, p1, p2, p3, keep_ref, send_ref, up_s):
    parts = (p0, p1, p2, p3)
    up_s[...] = product([a[0:768, :] for a in parts], [tiles(a, 768, 6) for a in parts])

    def chunk(block, target):
        at = pl.multiple_of(96 * block, 96)
        target[...] = up_s[pl.ds(at, 96), :].astype(target.dtype)

    place(sc, chunk, keep_ref, send_ref)


def third_kernel(sc, p0, p1, p2, p3, e0, e1, e2, e3, keep_ref, send_ref, res_s):
    parts = (p0, p1, p2, p3)
    res_s[...] = product([e[0:D, :] for e in (e0, e1, e2, e3)], [a[0:T, :] for a in parts])
    gains = sum(a[T : T + 8, :].astype(F32) for a in parts)

    def chunk(block, target):
        at = pl.multiple_of(96 * block, 96)
        target[0:96, :] = res_s[pl.ds(at, 96), :].astype(target.dtype)
        target[96:104, :] = gains.astype(target.dtype)

    place(sc, chunk, keep_ref, send_ref)


def weights(kernel, scalars, args, rows, width, scratch):
    outs = (sds((4, rows, width), F32), sds((4, rows, width), BF))
    return call(
        kernel, scalars, args, [whole(a.shape) for a in args], outs, [whole(o.shape) for o in outs], (1,),
        [pltpu.VMEM(shape, F32) for shape in scratch], vmem=8, flops=600_000_000, size=5_000_000,
    )


def spread_kernel(fill, sc, *refs):
    for k, part in enumerate(refs[0:4]):
        quarter = sc[6] ^ k
        for j in range(4):
            @pl.when(quarter == j)
            def _():
                fill(j, part, *refs[4:])


def spread(fill, scalars, parts, shapes):
    outs = tuple(sds(shape, F32) for shape in shapes)
    return call(
        functools.partial(spread_kernel, fill), scalars, parts, [whole(a.shape) for a in parts], outs,
        [whole(o.shape) for o in outs], (1,), vmem=4, size=2_000_000,
    )


def fill_first(j, part, down_ref, out_ref):
    down_ref[96 * j : 96 * j + 96, :] = part[0:96, :].astype(F32)
    row, col = 48 * (j >> 1), 384 * (j & 1)
    out_ref[row : row + 24, col : col + 384] = part[96:120, 0:384].astype(F32)
    out_ref[row + 24 : row + 48, col : col + 384] = part[96:120, 384:768].astype(F32)


def fill_second(j, part, up_ref):
    up_ref[:, 768 * j : 768 * j + 768] = part[...].astype(F32)


def fill_third(j, part, qkv_ref, gain_ref):
    skip = 128 if j >= 2 else 0
    begin = 0 if j == 0 else 128 * (4 * j + 1)
    qkv_ref[:, begin + skip : begin + WIN] = part[0:96, skip:WIN].astype(F32)
    if j == 0:
        gain_ref[...] = part[96:104, :].astype(F32)


def swap(array, axis, bits):
    size = lax.axis_size(axis)
    return lax.ppermute(array, axis, [(i, i ^ bits) for i in range(size)])


def reduce_spans(keep, send, steps=(1, 2, 4)):
    for bits in steps:
        total = keep + swap(send, "seq", bits).astype(F32)
        half = total.shape[0] // 2
        if half:
            keep, send = total[:half], total[half:].astype(BF)
    return total[0].astype(BF)


def per_device_fast(
    tokens, lengths, buckets, feature_proj, attn_gain, qkv_weight, out_weight, mlp_gain, up_weight,
    down_weight, cotangent,
):
    seq, row = lax.axis_index("seq"), lax.axis_index("dp")
    spans = lax.axis_size("seq")
    token_order, grad_order = (1, 2, 3, 4, 6, 5, 7), (2, 4, 6, 1, 3, 5, 7)
    before, after = seq ^ jnp.maximum(seq - 1, 0), seq ^ jnp.minimum(seq + 1, spans - 1)
    scalars = jnp.stack(
        [
            seq, lengths[0], jnp.maximum(before - 1, 0), jnp.maximum(after - 1, 0),
            seq > 0, seq < spans - 1, row,
            jnp.where(after == 7, 7, jnp.where(after == 3, 5, 4)),
            *[seq ^ k for k in token_order], *[0] * 9,
            *[seq ^ k for k in grad_order], *[0] * 9,
            *[token_order.index(k) for k in grad_order],
        ]
    ).astype(jnp.int32)
    own, cot = tokens[0], cotangent[0]
    gain_in, gain_mid = attn_gain[None], mlp_gain[None]

    near, far_a, far_b, mate = (swap(own, "seq", bits) for bits in (2, 4, 6, 1))
    early, qkv, phi_q, phi_k, expo, blend, num, den, proj, tags = own_forward(
        scalars, own, gain_in, qkv_weight, feature_proj, cot, buckets[0]
    )
    near, early = lax.optimization_barrier((near, early))
    early_1, early_2 = swap(early, "dp", 1), swap(early, "dp", 2)
    tags_prev = from_behind(tags, "seq", 1)
    some = others_forward(
        scalars, 0, jnp.stack([mate, near, swap(near, "seq", 1)]), gain_in, qkv_weight, proj
    )
    far, some, late = lax.optimization_barrier((jnp.stack([far_a, far_b]), some, (early, early_1, early_2)))
    early_3 = swap(late[0], "dp", 3)
    u, v, phi, sums, norms = others_forward(
        scalars, 3, jnp.concatenate([far, swap(far, "seq", 1)], 0), gain_in, qkv_weight, proj, some
    )
    others = (u, v, phi)
    sums, early = lax.optimization_barrier((sums, (early, early_1, early_2, early_3)))
    results = middle(
        scalars, own, qkv, phi_q, sums, norms, num, den, tags, tags_prev, others, gain_mid, out_weight,
        up_weight, down_weight, cot,
    )
    pay_1, pay_2 = results[0:4], results[4:8]
    layer_out, dmid, dn_low, dnum, dden, expo_e, blend_e, gmlp = results[8:]
    dn_far = [swap(dn_low, "seq", bits) for bits in (2, 4, 6)]
    parts_1 = [pay_1[0], swap(pay_1[1], "dp", 1), swap(pay_1[2], "dp", 2)]
    dq, dk, dv, dphi = own_back(
        scalars, tags, tags_prev, qkv, phi_q, phi_k, proj, expo, blend, dnum, dden, sums, norms, others,
        expo_e, blend_e,
    )
    dn_half, parts_1, last_1, dk = lax.optimization_barrier(
        (jnp.stack([dn_low, *dn_far]), parts_1, pay_1[3], dk)
    )
    parts_1.append(swap(last_1, "dp", 3))
    dn_pieces = jnp.concatenate([dn_half, swap(dn_half, "seq", 1)], 0)
    parts_1, pay_2 = lax.optimization_barrier((parts_1, pay_2))
    parts_2 = [pay_2[0]] + [swap(pay_2[k], "dp", k) for k in (1, 2, 3)]
    keep, send = weights(first_kernel, scalars, (*parts_1, *early), ROWS_1, D, [(D, D), (384, 384)])
    total_1 = keep + swap(send, "seq", 1).astype(F32)
    total_1, dn_pieces = lax.optimization_barrier((total_1, dn_pieces))
    *pay_3, grad_tokens = last(
        scalars, dn_pieces, others, own, tags, qkv, phi_k, proj, dq, dk, dv, dphi, dmid, gain_in,
        qkv_weight, gmlp,
    )
    pay_3, parts_2 = lax.optimization_barrier((pay_3, parts_2))
    share_1 = reduce_spans(total_1[0:2], total_1[2:4].astype(BF), (2, 4))
    parts_3 = [pay_3[0]] + [swap(pay_3[k], "dp", k) for k in (1, 2, 3)]
    share_2 = reduce_spans(*weights(second_kernel, scalars, parts_2, ROWS_2, D, [(D, D)]))
    share_3 = reduce_spans(*weights(third_kernel, scalars, (*parts_3, *early), ROWS_B, WIN, [(D, WIN)]))

    def everywhere(share):
        return [share] + [swap(share, "dp", k) for k in (1, 2, 3)]

    down, out = spread(fill_first, scalars, everywhere(share_1), [(384, D), (96, D)])
    (up,) = spread(fill_second, scalars, everywhere(share_2), [(96, 4 * D)])
    grad_qkv, gains = spread(fill_third, scalars, everywhere(share_3), [(96, 3 * D), (8, WIN)])
    gains = gains[0:4].reshape(2, 2 * WIN)[:, 0:D]
    mine = lax.dynamic_slice_in_dim(gains, seq * 96, 96, 1)
    return (
        layer_out[None], grad_tokens[None], grad_qkv, out, up, down, mine[0], mine[1],
    )


SPARSE_BLOCK = 64


HIGH_PRECISION = lax.Precision.HIGHEST
FLOAT = jnp.float32
HALF = jnp.bfloat16


def from_behind(array, axis, by):
    size = lax.axis_size(axis)
    pairs = [(i, i + by) for i in range(size) if 0 <= i + by < size]
    return lax.ppermute(array, axis, pairs)


def prefix(value, axis, join, neutral, backward):
    count, mine = (lax.axis_size(axis), lax.axis_index(axis))
    pieces = jax.tree.map(lambda part: lax.all_gather(part, axis), value)
    if backward:
        pieces = jax.tree.map(lambda part: part[::-1], pieces)
        mine = count - 1 - mine
    so_far = jax.tree.map(
        lambda part, zero: jnp.full_like(part, 0) + jnp.asarray(zero, part.dtype), value, neutral
    )

    def hop(position, so_far):
        longer = join(so_far, jax.tree.map(lambda part: part[position], pieces))
        return jax.tree.map(lambda new, old: jnp.where(position < mine, new, old), longer, so_far)

    return lax.fori_loop(0, count - 1, hop, so_far)


def shortened(array):

    def short(part):
        return part.astype(jnp.bfloat16) if part.dtype == jnp.float32 else part

    return jax.tree.map(short, array)


def layer_norm(value_rows, gain):
    center = value_rows - jnp.mean(value_rows, -1, keepdims=True)
    spread = jnp.mean(center * center, -1, keepdims=True)
    return center * lax.rsqrt(spread + EPS) * gain


def feature_map(inputs, feature_proj):
    factor = feature_proj.shape[0] ** (-0.25)
    linear = jnp.einsum("rlhd,dm->rlhm", inputs, feature_proj, precision=HIGH_PRECISION) * factor
    square = 0.5 * factor * factor * jnp.sum(inputs * inputs, -1, keepdims=True)
    return jnp.exp(linear - square) * feature_proj.shape[1] ** (-0.5)


def feature_back(inputs, phi_vals, upstream, feature_proj):
    factor = feature_proj.shape[0] ** (-0.25)
    weighted = upstream * phi_vals
    linear = jnp.einsum("rlhm,dm->rlhd", weighted, feature_proj, precision=HIGH_PRECISION) * factor
    return linear - factor * factor * inputs * jnp.sum(weighted, -1, keepdims=True)


def add_pair(first, second):
    return (first[0] + second[0], first[1] + second[1])


def attention_parts(query, keys, tag_window, lengths, feature_proj, first_pos):
    tok_count = query.shape[1]
    key_count = keys.shape[1]
    query_pos = first_pos + jnp.arange(tok_count, dtype=jnp.int32)
    key_pos = first_pos - SPARSE_BLOCK + jnp.arange(key_count, dtype=jnp.int32)
    query_ok = query_pos[None, :] < lengths[:, None]
    key_ok = (key_pos[None, :] >= 0) & (key_pos[None, :] < lengths[:, None])
    own_flag = jnp.arange(key_count) >= SPARSE_BLOCK
    causal = key_pos[None, :] <= query_pos[:, None]
    near_block = key_pos[None, :] // SPARSE_BLOCK >= query_pos[:, None] // SPARSE_BLOCK - 1
    allowed = causal[None, None] & key_ok[:, None, None, :]
    matched = (
        (tag_window[:, :, SPARSE_BLOCK:, None] == tag_window[:, :, None, :])
        & allowed
        & near_block[None, None]
    )
    phi_query = feature_map(query.astype(FLOAT), feature_proj)
    phi_keys = feature_map(keys.astype(FLOAT), feature_proj)
    query_features = phi_query.astype(HALF)
    feat_keys = phi_keys.astype(HALF)
    scores = jnp.einsum(
        "rthd,rjhd->rhtj", query, keys, preferred_element_type=FLOAT
    ) * feature_proj.shape[0] ** (-0.5)
    exponent = jnp.exp(scores)
    approx = jnp.einsum("rthm,rjhm->rhtj", query_features, feat_keys, preferred_element_type=FLOAT)
    blended = jnp.where(
        matched,
        jnp.where(own_flag, exponent, exponent - approx),
        jnp.where(own_flag & allowed, approx, 0.0),
    )
    return (
        query_ok,
        key_ok,
        own_flag,
        allowed,
        matched,
        phi_query,
        phi_keys,
        query_features,
        feat_keys,
        exponent,
        blended,
    )


def per_device(
    tokens,
    lengths,
    buckets,
    feature_proj,
    attn_gain,
    qkv_weight,
    out_weight,
    mlp_gain,
    up_weight,
    down_weight,
    cotangent,
):
    row_count, tok_count, model_width = tokens.shape
    head_count = buckets.shape[1]
    head_size = model_width // head_count
    resid = tokens.astype(FLOAT)
    normed_in = layer_norm(resid, attn_gain).astype(HALF)
    projected = jnp.dot(normed_in, qkv_weight, preferred_element_type=FLOAT).astype(HALF)
    shaped = projected.reshape(row_count, tok_count, 3, head_count, head_size)
    query = shaped[:, :, 0]
    own_keys = shaped[:, :, 1]
    own_values = shaped[:, :, 2]
    tags = buckets.astype(HALF)
    edge_keys, edge_values, edge_tags = from_behind(
        (own_keys[:, -SPARSE_BLOCK:], own_values[:, -SPARSE_BLOCK:], tags[:, :, -SPARSE_BLOCK:]),
        "seq",
        1,
    )
    keys = jnp.concatenate([edge_keys, own_keys], 1)
    value_rows = jnp.concatenate([edge_values, own_values], 1)
    tag_window = jnp.concatenate([edge_tags, tags], 2)
    first_pos = lax.axis_index("seq") * tok_count
    (
        query_ok,
        key_ok,
        own_flag,
        allowed,
        matched,
        phi_query,
        phi_keys,
        query_features,
        feat_keys,
        exponent,
        blended,
    ) = attention_parts(query, keys, tag_window, lengths, feature_proj, first_pos)
    retained_features = jnp.where(
        key_ok[:, SPARSE_BLOCK:, None, None],
        feat_keys[:, SPARSE_BLOCK:],
        jnp.zeros_like(feat_keys[:, SPARSE_BLOCK:]),
    )
    sum_add = jnp.einsum(
        "rthm,rthd->rhmd", retained_features, own_values, preferred_element_type=FLOAT
    )
    norm_add = jnp.sum(retained_features.astype(FLOAT), 1)
    zero_sums = jnp.zeros_like(sum_add)
    zero_norms = jnp.zeros_like(norm_add)
    running_feature_sums, carry_norms = prefix(
        (sum_add, norm_add), "seq", add_pair, (zero_sums, zero_norms), False
    )
    feat_query_f = query_features.astype(FLOAT)
    blended_low = blended.astype(HALF)
    attention_numerator = jnp.einsum(
        "rthm,rhmd->rthd", feat_query_f, running_feature_sums, precision=HIGH_PRECISION
    )
    attention_numerator = attention_numerator + jnp.einsum(
        "rhtj,rjhd->rthd", blended_low, value_rows, preferred_element_type=FLOAT
    )
    denominator = jnp.einsum(
        "rthm,rhm->rth", feat_query_f, carry_norms, precision=HIGH_PRECISION
    ) + jnp.sum(blended, -1).transpose(0, 2, 1)
    den_safe = jnp.where(query_ok[..., None], denominator, 1.0)
    attended = jnp.where(query_ok[..., None, None], attention_numerator / den_safe[..., None], 0.0)
    attended_low = attended.reshape(row_count, tok_count, model_width).astype(HALF)
    mid_resid = resid + jnp.dot(attended_low, out_weight, preferred_element_type=FLOAT)
    normed_mid = layer_norm(mid_resid, mlp_gain).astype(HALF)
    pre_act = jnp.dot(normed_mid, up_weight, preferred_element_type=FLOAT)
    hidden = jax.nn.gelu(pre_act, approximate=True).astype(HALF)
    layer_out = (mid_resid + jnp.dot(hidden, down_weight, preferred_element_type=FLOAT)).astype(
        HALF
    )
    upstream = cotangent.astype(FLOAT)
    grad_down = jnp.einsum("rtf,rtd->fd", hidden, cotangent, preferred_element_type=FLOAT)
    grad_hidden = jnp.einsum("rtd,fd->rtf", cotangent, down_weight, preferred_element_type=FLOAT)
    gelu_vals, gelu_pull = jax.vjp(lambda inner: jax.nn.gelu(inner, approximate=True), pre_act)
    grad_pre = gelu_pull(grad_hidden)[0].astype(HALF)
    grad_up = jnp.einsum("rtd,rtf->df", normed_mid, grad_pre, preferred_element_type=FLOAT)
    grad_normed_mid = jnp.einsum("rtf,df->rtd", grad_pre, up_weight, preferred_element_type=FLOAT)
    mid_vals, mid_pull = jax.vjp(layer_norm, mid_resid, mlp_gain)
    grad_mid_part, grad_mlp_gain = mid_pull(grad_normed_mid)
    grad_mid = upstream + grad_mid_part
    grad_out = jnp.einsum(
        "rtd,rte->de", attended_low.astype(FLOAT), grad_mid, precision=HIGH_PRECISION
    )
    grad_att = jnp.einsum(
        "rte,de->rtd", grad_mid, out_weight.astype(FLOAT), precision=HIGH_PRECISION
    ).astype(HALF)
    grad_att = grad_att.astype(FLOAT).reshape(row_count, tok_count, head_count, head_size)
    grad_numer = jnp.where(query_ok[..., None, None], grad_att / den_safe[..., None], 0.0)
    grad_denom = -jnp.sum(grad_numer * attention_numerator, -1) / den_safe
    grad_feat_query = (
        jnp.einsum("rthd,rhmd->rthm", grad_numer, running_feature_sums, precision=HIGH_PRECISION)
        + grad_denom[..., None] * carry_norms[:, None]
    )
    grad_carry_sums = jnp.einsum(
        "rthm,rthd->rhmd", feat_query_f, grad_numer, precision=HIGH_PRECISION
    )
    grad_carry_norms = jnp.einsum(
        "rthm,rth->rhm", feat_query_f, grad_denom, precision=HIGH_PRECISION
    )
    later_sums, later_norms = prefix(
        (grad_carry_sums, grad_carry_norms), "seq", add_pair, (zero_sums, zero_norms), True
    )
    grad_blend = (
        jnp.einsum(
            "rthd,rjhd->rhtj", grad_numer, value_rows.astype(FLOAT), precision=HIGH_PRECISION
        )
        + grad_denom.transpose(0, 2, 1)[..., None]
    )
    grad_values = jnp.einsum(
        "rhtj,rthd->rjhd", blended_low.astype(FLOAT), grad_numer, precision=HIGH_PRECISION
    )
    grad_expo = jnp.where(matched, grad_blend, 0.0)
    grad_approx = jnp.where(
        matched,
        jnp.where(own_flag, 0.0, -grad_blend),
        jnp.where(own_flag & allowed, grad_blend, 0.0),
    )
    grad_scores = grad_expo * exponent * head_size ** (-0.5)
    grad_query = jnp.einsum(
        "rhtj,rjhd->rthd", grad_scores, keys.astype(FLOAT), precision=HIGH_PRECISION
    )
    grad_keys = jnp.einsum(
        "rhtj,rthd->rjhd", grad_scores, query.astype(FLOAT), precision=HIGH_PRECISION
    )
    grad_feat_query = grad_feat_query + jnp.einsum(
        "rhtj,rjhm->rthm", grad_approx, feat_keys.astype(FLOAT), precision=HIGH_PRECISION
    )
    grad_feat_keys = jnp.einsum(
        "rhtj,rthm->rjhm", grad_approx, feat_query_f, precision=HIGH_PRECISION
    )
    own_mask = key_ok[:, SPARSE_BLOCK:, None, None]
    carry_feat = (
        jnp.einsum(
            "rthd,rhmd->rthm", own_values.astype(FLOAT), later_sums, precision=HIGH_PRECISION
        )
        + later_norms[:, None]
    )
    carry_vals = jnp.einsum(
        "rthm,rhmd->rthd",
        feat_keys[:, SPARSE_BLOCK:].astype(FLOAT),
        later_sums,
        precision=HIGH_PRECISION,
    )
    grad_feat_keys = jnp.concatenate(
        [
            grad_feat_keys[:, :SPARSE_BLOCK],
            grad_feat_keys[:, SPARSE_BLOCK:] + jnp.where(own_mask, carry_feat, 0.0),
        ],
        1,
    )
    grad_values = jnp.concatenate(
        [
            grad_values[:, :SPARSE_BLOCK],
            grad_values[:, SPARSE_BLOCK:] + jnp.where(own_mask, carry_vals, 0.0),
        ],
        1,
    )
    grad_query = grad_query + feature_back(
        query.astype(FLOAT), phi_query, grad_feat_query, feature_proj
    )
    grad_keys = grad_keys + feature_back(keys.astype(FLOAT), phi_keys, grad_feat_keys, feature_proj)
    back_keys, back_values = from_behind(
        (shortened(grad_keys[:, :SPARSE_BLOCK]), shortened(grad_values[:, :SPARSE_BLOCK])),
        "seq",
        -1,
    )
    own_grad_keys = grad_keys[:, SPARSE_BLOCK:]
    own_grad_values = grad_values[:, SPARSE_BLOCK:]
    own_grad_keys = jnp.concatenate(
        [
            own_grad_keys[:, : tok_count - SPARSE_BLOCK],
            own_grad_keys[:, tok_count - SPARSE_BLOCK :] + back_keys,
        ],
        1,
    )
    own_grad_values = jnp.concatenate(
        [
            own_grad_values[:, : tok_count - SPARSE_BLOCK],
            own_grad_values[:, tok_count - SPARSE_BLOCK :] + back_values,
        ],
        1,
    )
    grad_proj = (
        jnp.stack([grad_query, own_grad_keys, own_grad_values], 2)
        .reshape(row_count, tok_count, 3 * model_width)
        .astype(HALF)
    )
    grad_qkv = jnp.einsum("rtd,rte->de", normed_in, grad_proj, preferred_element_type=FLOAT)
    grad_normed_in = jnp.einsum("rte,de->rtd", grad_proj, qkv_weight, preferred_element_type=FLOAT)
    in_vals, in_pull = jax.vjp(layer_norm, resid, attn_gain)
    grad_in_part, grad_attn_gain = in_pull(grad_normed_in)
    grad_tokens = grad_mid + grad_in_part
    shares = (
        lax.psum_scatter(grad_qkv, "seq", scatter_dimension=0, tiled=True),
        lax.psum_scatter(grad_out, "seq", scatter_dimension=0, tiled=True),
        lax.psum_scatter(grad_up, "seq", scatter_dimension=0, tiled=True),
        lax.psum_scatter(grad_down, "seq", scatter_dimension=0, tiled=True),
        lax.psum_scatter(grad_attn_gain, "seq", scatter_dimension=0, tiled=True),
        lax.psum_scatter(grad_mlp_gain, "seq", scatter_dimension=0, tiled=True),
    )
    totals = lax.psum((shares[0], shares[1], shares[2], shares[3], shares[4], shares[5]), "dp")
    return (
        layer_out,
        grad_tokens,
        totals[0],
        totals[1],
        totals[2],
        totals[3],
        totals[4],
        totals[5],
    )


def solution(mesh):
    in_specs = (
        P("dp", "seq", None),
        P("dp"),
        P("dp", None, "seq"),
        P(),
        P(),
        P(),
        P(),
        P(),
        P(),
        P(),
        P("dp", "seq", None),
    )
    out_specs = (
        P("dp", "seq", None),
        P("dp", "seq", None),
        P("seq", None),
        P("seq", None),
        P("seq", None),
        P("seq", None),
        P("seq"),
        P("seq"),
    )
    shape = dict(mesh.shape)
    fast = shape == {"dp": 4, "seq": 8}
    return jax.shard_map(
        per_device_fast if fast else per_device, mesh=mesh, in_specs=in_specs, out_specs=out_specs, check_vma=False
    )
```

```python
import functools

import jax
import jax.numpy as jnp
from jax import lax
from jax.experimental import pallas as pl
from jax.experimental.pallas import tpu as pltpu
from jax.sharding import PartitionSpec as P

EPS = 1e-05
F32 = jnp.float32
BF = jnp.bfloat16
T = 128
D = 768
H = 12
HD = 64
M = 256
HM = H * M
PAIRS = H // 2
EDGE = 64
WIN = 640
ROWS_1 = 120
ROWS_2 = 96
ROWS_B = 104
MIB = 1 << 20


def nn(a, b):
    return lax.dot_general(a, b, (((1,), (0,)), ((), ())), preferred_element_type=F32)


def nt(a, b):
    return lax.dot_general(a, b, (((1,), (1,)), ((), ())), preferred_element_type=F32)


def tn(a, b):
    return lax.dot_general(a, b, (((0,), (0,)), ((), ())), preferred_element_type=F32)


def split(a):
    high = a.astype(BF)
    return high, (a - high.astype(F32)).astype(BF)


def iota(shape, axis):
    return lax.broadcasted_iota(jnp.int32, shape, axis)


def lanes(*parts):
    return jnp.concatenate(parts, axis=1)


def norm_parts(value):
    center = value - jnp.mean(value, -1, keepdims=True)
    scale = lax.rsqrt(jnp.mean(center * center, -1, keepdims=True) + EPS)
    return center * scale, scale


def norm_back(unit, scale, gain, upstream):
    inner = upstream * gain
    return scale * (
        inner
        - jnp.mean(inner, -1, keepdims=True)
        - unit * jnp.mean(inner * unit, -1, keepdims=True)
    )


def phi_pair(pair, proj):
    linear = nn(lanes(pair, pair), proj)
    wide = pair.astype(F32)
    square = wide * wide
    first = iota(square.shape, 1) < HD
    out = []
    for half in range(2):
        mine = first if half == 0 else ~first
        total = jnp.sum(jnp.where(mine, square, 0.0), -1, keepdims=True)
        out.append(
            jnp.exp(linear[:, half * M : half * M + M] - total * (0.5 * HD**-0.5)) * M**-0.5
        )
    return out


def phi_back(pair, grads, phis, proj):
    weighted = [grad * phi for grad, phi in zip(grads, phis)]
    joined = lanes(*weighted)
    high, low = split(joined)
    linear = nt(high, proj[:128]) + nt(high, proj[128:]) + nt(low, proj[:128])
    sums = [jnp.sum(part, -1, keepdims=True) for part in weighted]
    first = iota(pair.shape, 1) < HD
    return linear - HD**-0.5 * pair.astype(F32) * jnp.where(first, sums[0], sums[1])


def pick(first, two):
    return jnp.where(first, two[0], two[1])


def masked(first, half, value):
    zero = jnp.zeros_like(value)
    return jnp.where(first, value, zero) if half == 0 else jnp.where(first, zero, value)


def columns_to(acc, head, column):
    return jnp.where(iota(acc.shape, 1) == head, column, acc)


def rounded(value):
    return value.astype(BF)


def call(kernel, scalars, args, in_specs, outs, out_specs, grid, scratch=(), flops=0, size=0, vmem=48, aliases=None):
    return pl.pallas_call(
        kernel,
        out_shape=outs,
        grid_spec=pltpu.PrefetchScalarGridSpec(
            num_scalar_prefetch=1,
            grid=grid,
            in_specs=in_specs,
            out_specs=out_specs,
            scratch_shapes=list(scratch),
        ),
        input_output_aliases=aliases or {},
        compiler_params=pltpu.CompilerParams(vmem_limit_bytes=vmem * MIB),
        cost_estimate=pl.CostEstimate(flops=flops // 1000, bytes_accessed=size // 1000, transcendentals=0),
    )(scalars, *args)


def whole(shape):
    return pl.BlockSpec(memory_space=pltpu.VMEM)


def sds(shape, dtype):
    return jax.ShapeDtypeStruct(shape, dtype)


def projection(feature_proj):
    scaled = feature_proj * HD ** (-0.25)
    high, low = split(scaled)
    none = jnp.zeros((HD, M), BF)
    return jnp.concatenate([lanes(high, none), lanes(none, high), lanes(low, none), lanes(none, low)], 0)


def pack_kernel(sc, x_ref, tag_ref, out_ref):
    out_ref[0:T, :] = x_ref[...]
    tags = tag_ref[...].astype(F32)
    wide = [lanes(*[tags[h : h + 1, :] for h in range(6 * r, 6 * r + 6)]) for r in range(2)]
    out_ref[T : T + 8, :] = jnp.concatenate(wide + [jnp.zeros((6, D), F32)], 0).astype(BF)


def packed(scalars, own, tags):
    out = sds((T + 8, D), BF)
    return call(
        pack_kernel, scalars, (own, tags), [whole(own.shape), whole(tags.shape)], out, whole(out.shape), (1,),
        vmem=2,
    )


def tag_pair(ref):
    rows = jnp.concatenate([ref[...].astype(F32), jnp.zeros((4, T), F32)], 0)
    return rows, rows.T


def own_kernel(
    sc, x_ref, gain_ref, w_ref, feature_ref, g_ref, tag_ref,
    pay_ref, qkv_ref, phiq_ref, phik_ref, expo_ref, blend_ref, num_ref, den_ref, proj_ref,
):
    unit, _ = norm_parts(x_ref[0:T, :].astype(F32))
    normed = unit * gain_ref[...]
    low = normed.astype(BF)
    pay_ref[0:D, :] = normed.T.astype(BF)
    for t in range(6):
        pay_ref[D + 128 * t : D + 128 * t + 128, :] = g_ref[:, 128 * t : 128 * t + 128]
    qkv_ref[...] = nn(low, w_ref[...]).astype(BF)
    rows, cols = tag_pair(tag_ref)
    first = iota((T, 128), 1) < HD
    query_at, key_at = iota((T, T), 0), iota((T, T), 1)
    allowed = (key_at <= query_at) & (key_at + sc[0] * T < sc[1])
    dens = jnp.zeros((T, 128), F32)
    proj = projection(feature_ref[...])
    proj_ref[...] = proj
    for p in range(PAIRS):
        at = slice(128 * p, 128 * p + 128)
        query, key, value = (
            qkv_ref[:, part * D + 128 * p : part * D + 128 * p + 128] for part in range(3)
        )
        phi_q, phi_k = phi_pair(query, proj), phi_pair(key, proj)
        nums = []
        for half in range(2):
            h = 2 * p + half
            phiq_ref[:, M * h : M * h + M] = phi_q[half]
            phik_ref[:, M * h : M * h + M] = phi_k[half]
            expo = jnp.exp(nt(masked(first, half, query), key) * HD**-0.5)
            approx = nt(phi_q[half].astype(BF), phi_k[half].astype(BF))
            matched = allowed & (cols[:, h : h + 1] == rows[h : h + 1, :])
            blend = jnp.where(matched, expo, jnp.where(allowed, approx, 0.0))
            expo_ref[h] = jnp.where(matched, expo, 0.0)
            blend_ref[h] = blend.astype(BF)
            nums.append(nn(blend.astype(BF), value))
            dens = columns_to(dens, h, jnp.sum(blend, -1, keepdims=True))
        num_ref[:, at] = pick(first, nums)
    den_ref[...] = dens


def own_forward(scalars, own, gain, qkv_weight, feature_proj, cotangent, tags):
    outs = (
        sds((2 * D, 128), BF), sds((T, 3 * D), BF), sds((T, HM), F32), sds((T, HM), F32),
        sds((H, T, T), F32), sds((H, T, T), BF), sds((T, D), F32), sds((T, 128), F32),
        sds((2 * 128, 2 * M), BF),
    )
    args = (own, gain, qkv_weight, feature_proj, cotangent, tags)
    return call(
        own_kernel, scalars, args, [whole(a.shape) for a in args], outs,
        [whole(o.shape) for o in outs], (1,), vmem=6, flops=2_000_000_000, size=9_000_000,
    )


def others_kernel(begin, sc, x_ref, gain_ref, w_ref, proj_ref, *refs):
    tags_ref, u_ref, v_ref, phi_ref, sums_ref, norms_ref = refs[-6:]
    slot = pl.program_id(0)
    span = sc[8 + begin + slot]

    @pl.when(slot == 0)
    def _():
        if begin:
            sums_ref[...], norms_ref[...] = refs[4][...], refs[5][...]
        else:
            sums_ref[...] = jnp.zeros_like(sums_ref)
            norms_ref[...] = jnp.zeros_like(norms_ref)

    unit, _ = norm_parts(x_ref[0, 0:T, :].astype(F32))
    wide = x_ref[0, T : T + 8, :].astype(F32)
    rows = [wide[h // 6 : h // 6 + 1, 128 * (h % 6) : 128 * (h % 6) + 128] for h in range(H)]
    tags_ref[0] = jnp.concatenate(rows + [jnp.zeros((4, 128), F32)], 0)
    low = (unit * gain_ref[...]).astype(BF)
    earlier = span < sc[0]
    offset = pl.multiple_of(jnp.where(earlier, D, 0), D)
    u_ref[0] = nn(low, w_ref[:, pl.ds(offset, D)]).astype(BF)
    proj = proj_ref[...]
    for p in range(PAIRS):
        phis = phi_pair(u_ref[0, :, 128 * p : 128 * p + 128], proj)
        for half in range(2):
            h = 2 * p + half
            phi_ref[0, :, M * h : M * h + M] = phis[half].astype(BF)

    @pl.when(earlier)
    def _():
        value = nn(low, w_ref[:, 2 * D : 3 * D])
        v_ref[0] = value.astype(BF)
        valid = iota((D, T), 1) + span * T < sc[1]
        turned = jnp.where(valid, value.T, 0.0).astype(BF)
        for h in range(H):
            sums_ref[HD * h : HD * h + HD, :] += nn(
                turned[HD * h : HD * h + HD, :], phi_ref[0, :, M * h : M * h + M]
            )
        ones = jnp.where(iota((8, T), 1) + span * T < sc[1], 1.0, 0.0).astype(BF)
        norms_ref[...] += nn(ones, phi_ref[0])

    @pl.when(~earlier)
    def _():
        v_ref[0] = jnp.zeros((T, D), BF)


def others_forward(scalars, begin, pieces, gain, qkv_weight, proj, so_far=()):
    count, spans = pieces.shape[0], 7
    outs = (
        sds((spans, 16, T), F32), sds((spans, T, D), BF), sds((spans, T, D), BF), sds((spans, T, HM), BF),
        sds((D, M), F32), sds((8, HM), F32),
    )
    step = lambda i, sc: (begin + i, 0, 0)
    specs = [pl.BlockSpec((1, T + 8, D), lambda i, sc: (i, 0, 0))]
    specs += [whole(a.shape) for a in (gain, qkv_weight, proj)]
    aliases = {}
    if so_far:
        specs += [pl.BlockSpec(memory_space=pl.ANY)] * 4 + [whole(a.shape) for a in so_far[4:]]
        aliases = {5: 0, 6: 1, 7: 2, 8: 3}
    return call(
        functools.partial(others_kernel, begin), scalars, (pieces, gain, qkv_weight, proj, *so_far), specs,
        outs,
        [pl.BlockSpec((1, 16, T), step), pl.BlockSpec((1, T, D), step), pl.BlockSpec((1, T, D), step),
         pl.BlockSpec((1, T, HM), step), whole((D, M)), whole((8, HM))],
        (count,), vmem=8, flops=count * 600_000_000, size=count * 1_400_000 + 3_500_000, aliases=aliases,
    )


def own_cols(tags_ref):
    return tag_pair(tags_ref)[1].astype(BF)


def middle_kernel(
    sc, x_ref, qkv_ref, phiq_ref, sums_ref, norms_ref, numl_ref, denl_ref, tags_ref,
    tags_prev, up_prev, vp_prev, phi_prev, gain_ref, wo_ref, wup_ref, wdown_ref, g_ref,
    hid_ref, pre_ref, nm_ref, att_ref, out_ref, dmid_ref, dn_low_ref, dn_ref, dd_ref, expo_ref, blend_ref, gain_out,
    mid_s, nm_s, acc_s, dnm_s, num_s, den_s,
):
    step = pl.program_id(0)
    first = iota((T, 128), 1) < HD
    valid = iota((T, 1), 0) + sc[0] * T < sc[1]

    @pl.when(step == 0)
    def _():
        _, own = tag_pair(tags_ref)
        prev = tags_prev[0]
        prev_tag = [prev[h : h + 1, EDGE:T] for h in range(H)]
        edge_first = iota((EDGE, 128), 1) < HD
        edge_ok = (sc[4] > 0) & (iota((EDGE, EDGE), 1) + (sc[0] * T - EDGE) < sc[1])
        dens = denl_ref[...]
        zeros = jnp.zeros((EDGE, 128), F32)
        for p in range(PAIRS):
            at = slice(128 * p, 128 * p + 128)
            high, lowp = split(sums_ref[at, :])
            query = qkv_ref[0:EDGE, at]
            key, value = up_prev[0, :, at], vp_prev[0, :, at]
            nums = []
            for half in range(2):
                h = 2 * p + half
                hm = slice(M * h, M * h + M)
                phi_q = phiq_ref[:, hm].astype(BF)
                total = nt(phi_q, high) + nt(phi_q, lowp)
                den = jnp.sum(phi_q.astype(F32) * norms_ref[0:1, hm], -1, keepdims=True)
                expo = jnp.exp(nt(masked(edge_first, half, query), key) * HD**-0.5)
                approx = nt(phi_q[0:EDGE], phi_prev[0, :, hm])
                matched = edge_ok & (own[0:EDGE, h : h + 1] == prev_tag[h])
                blend = jnp.where(matched, expo - approx, 0.0)
                expo_ref[h] = jnp.where(matched, expo, 0.0)
                blend_ref[h] = blend.astype(BF)
                total = total + jnp.concatenate([nn(blend.astype(BF), value), zeros], 0)
                den = den + jnp.concatenate(
                    [jnp.sum(blend, -1, keepdims=True), jnp.zeros((EDGE, 1), F32)], 0
                )
                nums.append(total)
                dens = jnp.where(iota(dens.shape, 1) == h, dens + den, dens)
            num_s[:, at] = numl_ref[:, at] + pick(first, nums)
        dens = jnp.where(valid, dens, 1.0)
        den_s[...] = dens
        for p in range(PAIRS):
            at = slice(128 * p, 128 * p + 128)
            den = jnp.where(first, dens[:, 2 * p : 2 * p + 1], dens[:, 2 * p + 1 : 2 * p + 2])
            mid_s[:, at] = jnp.where(valid, num_s[:, at] / den, 0.0)
        attended = mid_s[...].astype(BF)
        att_ref[...] = attended
        mid = x_ref[0:T, :].astype(F32) + nn(attended, wo_ref[...])
        mid_s[...] = mid
        unit, _ = norm_parts(mid)
        normed = unit * gain_ref[...]
        nm_s[...] = normed.astype(BF)
        nm_ref[...] = normed.astype(BF)
        acc_s[...] = jnp.zeros_like(acc_s)
        dnm_s[...] = jnp.zeros_like(dnm_s)

    pre = nn(nm_s[...], wup_ref[...])
    grad_hidden = nt(g_ref[...], wdown_ref[...])
    root = (2.0 / jnp.pi) ** 0.5
    inner = root * (pre + 0.044715 * (pre * pre * pre))
    tanh = jnp.tanh(inner)
    half_up = 0.5 * (1.0 + tanh)
    hidden = pre * half_up
    slope = half_up + 0.5 * pre * (1.0 - tanh * tanh) * (root * (1.0 + 3 * 0.044715 * (pre * pre)))
    grad_pre = (grad_hidden * slope).astype(BF)
    hidden_low = hidden.astype(BF)
    acc_s[...] += nn(hidden_low, wdown_ref[...])
    dnm_s[...] += nt(grad_pre, wup_ref[...])
    hid_ref[...] = hidden_low
    pre_ref[...] = grad_pre

    @pl.when(step == 3)
    def _():
        mid = mid_s[...]
        out_ref[...] = (mid + acc_s[...]).astype(BF)
        unit, scale = norm_parts(mid)
        grad = dnm_s[...]
        gain_out[...] = jnp.broadcast_to(jnp.sum(grad * unit, 0, keepdims=True), (8, D))
        dmid = g_ref[...].astype(F32) + norm_back(unit, scale, gain_ref[...], grad)
        dmid_ref[...] = dmid
        high, low = split(dmid)
        datt = (nt(high, wo_ref[...]) + nt(low, wo_ref[...])).astype(BF).astype(F32)
        dens = den_s[...]
        ddens = jnp.zeros((T, 128), F32)
        for p in range(PAIRS):
            at = slice(128 * p, 128 * p + 128)
            den = jnp.where(first, dens[:, 2 * p : 2 * p + 1], dens[:, 2 * p + 1 : 2 * p + 2])
            dnum = jnp.where(valid, datt[:, at] / den, 0.0)
            dn_ref[:, at] = dnum
            dn_low_ref[:, at] = dnum.astype(BF)
            prod = dnum * num_s[:, at]
            for half in range(2):
                h = 2 * p + half
                total = jnp.sum(masked(first, half, prod), -1, keepdims=True)
                ddens = columns_to(ddens, h, -total / dens[:, h : h + 1])
        dd_ref[...] = ddens
        dn_low_ref[:, D : D + 16] = ddens[:, 0:16].astype(BF)
        dn_low_ref[:, D + 16 : D + 32] = own_cols(tags_ref)
        dn_low_ref[:, D + 32 : D + 128] = jnp.zeros((T, 96), BF)


def middle(scalars, own, qkv, phi_q, sums, norms, num, den, tags, others, gain, wo, wup, wdown, cot):
    tags_all, u, v, phi = others
    prev = lambda i, sc: (sc[2], 1, 0)
    outs = (
        sds((T, 4 * D), BF), sds((T, 4 * D), BF), sds((T, D), BF), sds((T, D), BF),
        sds((T, D), BF), sds((T, D), F32), sds((T, D + 128), BF),
        sds((T, D), F32), sds((T, 128), F32), sds((H, EDGE, EDGE), F32), sds((H, EDGE, EDGE), BF),
        sds((8, D), F32),
    )
    args = (own, qkv, phi_q, sums, norms, num, den, tags, tags_all, u, v, phi, gain, wo, wup, wdown, cot)
    specs = [whole(a.shape) for a in args[:8]] + [
        pl.BlockSpec((1, 16, T), lambda i, sc: (sc[2], 0, 0)),
        pl.BlockSpec((1, EDGE, D), prev), pl.BlockSpec((1, EDGE, D), prev),
        pl.BlockSpec((1, EDGE, HM), prev),
        whole(gain.shape), whole(wo.shape),
        pl.BlockSpec((D, D), lambda i, sc: (0, i)), pl.BlockSpec((D, D), lambda i, sc: (i, 0)),
        whole(cot.shape),
    ]
    scratch = [
        pltpu.VMEM((T, D), F32), pltpu.VMEM((T, D), BF), pltpu.VMEM((T, D), F32),
        pltpu.VMEM((T, D), F32), pltpu.VMEM((T, D), F32), pltpu.VMEM((T, 128), F32),
    ]
    return call(
        middle_kernel, scalars, args, specs, outs,
        [pl.BlockSpec((T, D), lambda i, sc: (0, i))] * 2 + [whole(o.shape) for o in outs[2:]], (4,), scratch,
        vmem=12, flops=3_500_000_000, size=20_000_000,
    )


def exchange_kernel(sc, hid_ref, pre_ref, nm_ref, att_ref, dmid_ref, *refs):
    first_pay, second_pay, turn_s = refs[0:4], refs[4:8], refs[8]
    me = sc[6]
    for b in range(4):
        turn_s[D * b : D * b + D, :] = hid_ref[:, D * b : D * b + D].astype(F32).T.astype(BF)
    turned_nm = nm_ref[...].astype(F32).T.astype(BF)
    turned_att = att_ref[...].astype(F32).T.astype(BF)
    dmid = dmid_ref[...].astype(BF)
    for k in range(4):
        mate = me ^ k
        for s in range(8):
            begin = pl.multiple_of(384 * s + 96 * mate, 96)
            first_pay[k][96 * s : 96 * s + 96, :] = turn_s[pl.ds(begin, 96), :]
            first_pay[k][768 + 48 * s : 768 + 48 * s + 48, :] = jnp.where(
                mate >= 2, turned_att[96 * s + 48 : 96 * s + 96, :], turned_att[96 * s : 96 * s + 48, :]
            )
        for t in range(3):
            first_pay[k][1152 + 128 * t : 1152 + 128 * t + 128, :] = jnp.where(
                (mate & 1) > 0, dmid[:, 384 + 128 * t : 512 + 128 * t], dmid[:, 128 * t : 128 * t + 128]
            )
        second_pay[k][0:D, :] = turned_nm
        for t in range(6):
            begin = pl.multiple_of(D * mate + 128 * t, 128)
            second_pay[k][D + 128 * t : D + 128 * t + 128, :] = pre_ref[:, pl.ds(begin, 128)]


def exchange(scalars, *args):
    outs = tuple([sds((2 * D, 128), BF)] * 8)
    return call(
        exchange_kernel, scalars, args, [whole(a.shape) for a in args], outs, [whole(o.shape) for o in outs],
        (1,), [pltpu.VMEM((4 * D, T), BF)], vmem=8,
    )


def own_back_kernel(
    sc, tags_ref, qkv_ref, phiq_ref, phik_ref, proj_ref, expo_ref, blend_ref, dn_ref, dd_ref,
    sums_ref, norms_ref, tags_prev, up_prev, vp_prev, phi_prev, expo_e, blend_e,
    dq_ref, dk_ref, dv_ref, dphi_ref,
):
    rows, cols = tag_pair(tags_ref)
    first = iota((T, 128), 1) < HD
    query_at, key_at = iota((T, T), 0), iota((T, T), 1)
    allowed = (key_at <= query_at) & (key_at + sc[0] * T < sc[1])
    prev_tag = tags_prev[0]
    edge_first = iota((EDGE, 128), 1) < HD
    edge_ok = (sc[4] > 0) & (iota((EDGE, EDGE), 1) + (sc[0] * T - EDGE) < sc[1])
    proj = proj_ref[...]
    for p in range(PAIRS):
        at = slice(128 * p, 128 * p + 128)
        query, key, value = (
            qkv_ref[:, part * D + 128 * p : part * D + 128 * p + 128] for part in range(3)
        )
        key_e, value_e = up_prev[0, :, at], vp_prev[0, :, at]
        high, low = split(dn_ref[:, at])
        both = lanes(high, low)
        s_high, s_low = split(sums_ref[at, :])
        grads, phis, dqs, dks, dvs = [], [], [], [], []
        for half in range(2):
            h = 2 * p + half
            hm = slice(M * h, M * h + M)
            dden = dd_ref[:, h : h + 1]
            mine = lanes(masked(first, half, high), masked(first, half, low))
            phi_q, phi_k = phiq_ref[:, hm], phik_ref[:, hm]
            dw = nt(mine, lanes(value, value)) + dden
            matched = cols[:, h : h + 1] == rows[h : h + 1, :]
            ds = (dw * expo_ref[h] * HD**-0.5).astype(BF)
            da = jnp.where(allowed & ~matched, dw, 0.0).astype(BF)
            dq = nn(ds, key)
            dks.append(tn(ds, query))
            dv = tn(blend_ref[h], both)
            dvs.append(dv[:, 0:128] + dv[:, 128:256])
            dphi = nn(da, phi_k.astype(BF)) + dden * norms_ref[0:1, hm]
            dphi = dphi + nn(mine, jnp.concatenate([s_high, s_high], 0))
            dphi = dphi + nn(mine[:, 0:128], s_low)
            dphi_ref[:, hm] = tn(da, phi_q.astype(BF))
            edge = nt(mine[0:EDGE], lanes(value_e, value_e)) + dden[0:EDGE]
            matched_e = edge_ok & (cols[0:EDGE, h : h + 1] == prev_tag[h : h + 1, EDGE:T])
            ds_e = (edge * expo_e[h] * HD**-0.5).astype(BF)
            da_e = jnp.where(matched_e, -edge, 0.0).astype(BF)
            dqs.append(dq + jnp.concatenate([nn(ds_e, key_e), jnp.zeros((EDGE, 128), F32)], 0))
            grads.append(
                dphi + jnp.concatenate([nn(da_e, phi_prev[0, :, hm]), jnp.zeros((EDGE, M), F32)], 0)
            )
            phis.append(phi_q)
        dq_ref[:, at] = (pick(first, dqs) + phi_back(query, grads, phis, proj)).astype(BF)
        dk_ref[:, at] = pick(first, dks)
        dv_ref[:, at] = pick(first, dvs)


def own_back(scalars, tags, qkv, phi_q, phi_k, proj, expo, blend, dnum, dden, sums, norms, others, expo_e, blend_e):
    tags_all, u, v, phi = others
    prev = lambda i, sc: (sc[2], 1, 0)
    args = (
        tags, qkv, phi_q, phi_k, proj, expo, blend, dnum, dden, sums, norms, tags_all, u, v, phi, expo_e,
        blend_e,
    )
    specs = [whole(a.shape) for a in args[:11]] + [
        pl.BlockSpec((1, 16, T), lambda i, sc: (sc[2], 0, 0)),
        pl.BlockSpec((1, EDGE, D), prev), pl.BlockSpec((1, EDGE, D), prev),
        pl.BlockSpec((1, EDGE, HM), prev),
        whole(expo_e.shape), whole(blend_e.shape),
    ]
    outs = (sds((T, D), BF), sds((T, D), F32), sds((T, D), F32), sds((T, HM), F32))
    return call(
        own_back_kernel, scalars, args, specs, outs, [whole(o.shape) for o in outs], (1,),
        vmem=8, flops=3_000_000_000, size=9_000_000,
    )


def last_kernel(
    sc, dn_slot, phi_slot, x_ref, tags_ref, qkv_ref, phik_ref, proj_ref, dq_ref, dk_ref, dv_ref, dphi_ref,
    u_next, phi_next, dn_next, dmid_ref, gain_ref, w_ref, gmlp_ref,
    a0, a1, a2, a3, grad_ref, sums_s, norms_s, dqkv_s,
):
    slot = pl.program_id(0)
    span = sc[24 + slot]

    @pl.when(slot == 0)
    def _():
        sums_s[...] = jnp.zeros_like(sums_s)
        norms_s[...] = jnp.zeros_like(norms_s)

    @pl.when(span > sc[0])
    def _():
        turned = dn_slot[0].astype(F32).T.astype(BF)
        for h in range(H):
            hm = slice(M * h, M * h + M)
            sums_s[HD * h : HD * h + HD, :] += nn(turned[HD * h : HD * h + HD, :], phi_slot[0, :, hm])
        norms_s[...] += nn(turned[D : D + 16, :], phi_slot[0])

    @pl.when(slot == pl.num_programs(0) - 1)
    def _():
        me = sc[6]
        rows = tags_ref[...].astype(F32)
        next_cols = dn_next[0, :, D + 16 : D + 32].astype(F32)
        first = iota((T, 128), 1) < HD
        edge_first = iota((EDGE, 128), 1) < HD
        valid = iota((T, 1), 0) + sc[0] * T < sc[1]
        edge_ok = (sc[5] > 0) & (iota((EDGE, EDGE), 1) + (sc[0] * T + EDGE) < sc[1])
        proj = proj_ref[...]
        ddn = dn_next[0, :, D : D + 128].astype(F32)
        dqkv_s[:, 0:D] = dq_ref[...]
        for p in range(PAIRS):
            at = slice(128 * p, 128 * p + 128)
            key, value = (qkv_ref[:, part * D + 128 * p : part * D + 128 * p + 128] for part in (1, 2))
            high, low = split(sums_s[at, :])
            query_n, dnum_n = u_next[0, :, at], dn_next[0, :, at]
            grads, phis, dks, dvs = [], [], [], []
            for half in range(2):
                h = 2 * p + half
                hm = slice(M * h, M * h + M)
                phi_k = phik_ref[:, hm]
                phi_kb = phi_k.astype(BF)
                mine = masked(first, half, value)
                carry = nn(mine, high) + nn(mine, low) + norms_s[h : h + 1, hm]
                dv = nt(phi_kb, high) + nt(phi_kb, low)
                q_h, d_h = masked(edge_first, half, query_n), masked(edge_first, half, dnum_n)
                phi_n = phi_next[0, :, hm]
                expo = jnp.exp(nt(q_h, key[EDGE:]) * HD**-0.5)
                approx = nt(phi_n, phi_kb[EDGE:])
                matched = edge_ok & (next_cols[0:EDGE, h : h + 1] == rows[h : h + 1, EDGE:128])
                blend = jnp.where(matched, expo - approx, 0.0).astype(BF)
                dw = nt(d_h, value[EDGE:]) + ddn[:, h : h + 1]
                ds = jnp.where(matched, dw * expo * HD**-0.5, 0.0).astype(BF)
                da = jnp.where(matched, -dw, 0.0).astype(BF)
                none = jnp.zeros((EDGE, 128), F32)
                dks.append(jnp.concatenate([none, tn(ds, query_n)], 0))
                dvs.append(jnp.where(valid, dv, 0.0) + jnp.concatenate([none, tn(blend, dnum_n)], 0))
                grads.append(
                    dphi_ref[:, hm] + jnp.where(valid, carry, 0.0)
                    + jnp.concatenate([jnp.zeros((EDGE, M), F32), tn(da, phi_n)], 0)
                )
                phis.append(phi_k)
            dqkv_s[:, D + 128 * p : D + 128 * p + 128] = (
                dk_ref[:, at] + pick(first, dks) + phi_back(key, grads, phis, proj)
            ).astype(BF)
            dqkv_s[:, 2 * D + 128 * p : 2 * D + 128 * p + 128] = (dv_ref[:, at] + pick(first, dvs)).astype(BF)
        grad = nt(dqkv_s[...], w_ref[...])
        unit, scale = norm_parts(x_ref[0:T, :].astype(F32))
        grad_ref[...] = dmid_ref[...] + norm_back(unit, scale, gain_ref[...], grad)
        attn = jnp.sum(grad * unit, 0, keepdims=True)
        mlp = gmlp_ref[0:1, :]
        row = iota((8, WIN), 0)
        gains = jnp.zeros((8, WIN), F32)
        tail = jnp.zeros((1, 2 * WIN - D), F32)
        for at, part in enumerate((attn, mlp)):
            gains = jnp.where(row == 2 * at, part[:, 0:WIN], gains)
            gains = jnp.where(row == 2 * at + 1, lanes(part[:, WIN:D], tail), gains)
        for k, pay_ref in enumerate((a0, a1, a2, a3)):
            mate = me ^ k
            begin = pl.multiple_of(jnp.where(mate == 0, 0, 128 * (4 * mate + 1)), 128)
            pay_ref[0:T, :] = dqkv_s[:, pl.ds(begin, WIN)]
            pay_ref[T : T + 8, :] = gains.astype(BF)


def last(scalars, dn_pieces, others, own, tags, qkv, phi_k, proj, dq, dk, dv, dphi, dmid, gain, qkv_weight, gmlp):
    _, u, v, phi = others
    count = dn_pieces.shape[0] - 1
    follow = lambda i, sc: (sc[3], 0, 0)
    args = (
        dn_pieces, phi, own, tags, qkv, phi_k, proj, dq, dk, dv, dphi, u, phi, dn_pieces, dmid, gain,
        qkv_weight, gmlp,
    )
    specs = [
        pl.BlockSpec((1, T, D + 128), lambda i, sc: (i + 1, 0, 0)),
        pl.BlockSpec((1, T, HM), lambda i, sc: (sc[40 + i], 0, 0)),
    ]
    specs += [whole(a.shape) for a in args[2:11]]
    specs += [
        pl.BlockSpec((1, EDGE, D), follow), pl.BlockSpec((1, EDGE, HM), follow),
        pl.BlockSpec((1, EDGE, D + 128), lambda i, sc: (sc[7], 0, 0)),
    ] + [whole(a.shape) for a in args[14:]]
    outs = tuple([sds((T + 8, WIN), BF)] * 4) + (sds((T, D), F32),)
    return call(
        last_kernel, scalars, args, specs, outs, [whole(o.shape) for o in outs], (count,),
        [pltpu.VMEM((D, M), F32), pltpu.VMEM((16, HM), F32), pltpu.VMEM((T, 3 * D), BF)],
        vmem=10, flops=3_000_000_000, size=count * 1_000_000 + 10_000_000,
    )


def reverse3(at):
    return ((at & 1) << 2) | (at & 2) | (at >> 2)


def place(sc, chunk_of, keep_ref, send_ref):
    for r in range(8):
        block = reverse3(r) ^ sc[0]
        target = keep_ref.at[r] if r < 4 else send_ref.at[r - 4]
        chunk_of(block, target)


def joined(parts, begin, size):
    return lanes(*[part[begin : begin + size, :] for part in parts])


def tiles(part, begin, count):
    return lanes(*[part[begin + 128 * t : begin + 128 * t + 128, :] for t in range(count)])


def product(lefts, rights):
    first = nn(lanes(lefts[0], lefts[1]), jnp.concatenate(rights[0:2], 0))
    return first + nn(lanes(lefts[2], lefts[3]), jnp.concatenate(rights[2:4], 0))


def first_kernel(sc, p0, p1, p2, p3, e0, e1, e2, e3, keep_ref, send_ref, down_s, out_s):
    parts = (p0, p1, p2, p3)
    cots = [e[D : 2 * D, :] for e in (e0, e1, e2, e3)]
    down_s[...] = product([a[0:768, :] for a in parts], [tiles(a, 0, 6) for a in cots])
    out_s[...] = product([a[768:1152, :] for a in parts], [tiles(a, 1152, 3) for a in parts])

    def chunk(block, target):
        at = pl.multiple_of(96 * block, 96)
        target[0:96, :] = down_s[pl.ds(at, 96), :].astype(target.dtype)
        at = pl.multiple_of(48 * block, 48)
        target[96:120, 0:384] = out_s[pl.ds(at, 24), :].astype(target.dtype)
        at = pl.multiple_of(48 * block + 24, 24)
        target[96:120, 384:768] = out_s[pl.ds(at, 24), :].astype(target.dtype)

    place(sc, chunk, keep_ref, send_ref)


def second_kernel(sc, p0, p1, p2, p3, keep_ref, send_ref, up_s):
    parts = (p0, p1, p2, p3)
    up_s[...] = product([a[0:768, :] for a in parts], [tiles(a, 768, 6) for a in parts])

    def chunk(block, target):
        at = pl.multiple_of(96 * block, 96)
        target[...] = up_s[pl.ds(at, 96), :].astype(target.dtype)

    place(sc, chunk, keep_ref, send_ref)


def third_kernel(sc, p0, p1, p2, p3, e0, e1, e2, e3, keep_ref, send_ref, res_s):
    parts = (p0, p1, p2, p3)
    res_s[...] = product([e[0:D, :] for e in (e0, e1, e2, e3)], [a[0:T, :] for a in parts])
    gains = sum(a[T : T + 8, :].astype(F32) for a in parts)

    def chunk(block, target):
        at = pl.multiple_of(96 * block, 96)
        target[0:96, :] = res_s[pl.ds(at, 96), :].astype(target.dtype)
        target[96:104, :] = gains.astype(target.dtype)

    place(sc, chunk, keep_ref, send_ref)


def weights(kernel, scalars, args, rows, width, scratch):
    outs = (sds((4, rows, width), F32), sds((4, rows, width), BF))
    return call(
        kernel, scalars, args, [whole(a.shape) for a in args], outs, [whole(o.shape) for o in outs], (1,),
        [pltpu.VMEM(shape, F32) for shape in scratch], vmem=8, flops=600_000_000, size=20_000_000_000,
    )


def spread_kernel(fill, sc, *refs):
    for k, part in enumerate(refs[0:4]):
        quarter = sc[6] ^ k
        for j in range(4):
            @pl.when(quarter == j)
            def _():
                fill(j, part, *refs[4:])


def spread(fill, scalars, parts, shapes):
    outs = tuple(sds(shape, F32) for shape in shapes)
    return call(
        functools.partial(spread_kernel, fill), scalars, parts, [whole(a.shape) for a in parts], outs,
        [whole(o.shape) for o in outs], (1,), vmem=4, size=2_000_000,
    )


def fill_first(j, part, down_ref, out_ref):
    down_ref[96 * j : 96 * j + 96, :] = part[0:96, :].astype(F32)
    row, col = 48 * (j >> 1), 384 * (j & 1)
    out_ref[row : row + 24, col : col + 384] = part[96:120, 0:384].astype(F32)
    out_ref[row + 24 : row + 48, col : col + 384] = part[96:120, 384:768].astype(F32)


def fill_second(j, part, up_ref):
    up_ref[:, 768 * j : 768 * j + 768] = part[...].astype(F32)


def fill_third(j, part, qkv_ref, gain_ref):
    skip = 128 if j >= 2 else 0
    begin = 0 if j == 0 else 128 * (4 * j + 1)
    qkv_ref[:, begin + skip : begin + WIN] = part[0:96, skip:WIN].astype(F32)
    if j == 0:
        gain_ref[...] = part[96:104, :].astype(F32)


def swap(array, axis, bits):
    size = lax.axis_size(axis)
    return lax.ppermute(array, axis, [(i, i ^ bits) for i in range(size)])


def reduce_spans(keep, send, steps=(1, 2, 4)):
    for bits in steps:
        total = keep + swap(send, "seq", bits).astype(F32)
        half = total.shape[0] // 2
        if half:
            keep, send = total[:half], total[half:].astype(BF)
    return total[0].astype(BF)


def per_device_fast(
    tokens, lengths, buckets, feature_proj, attn_gain, qkv_weight, out_weight, mlp_gain, up_weight,
    down_weight, cotangent,
):
    seq, row = lax.axis_index("seq"), lax.axis_index("dp")
    spans = lax.axis_size("seq")
    token_order, grad_order = (1, 2, 4, 6, 3, 5, 7), (2, 4, 6, 1, 3, 5, 7)
    before, after = seq ^ jnp.maximum(seq - 1, 0), seq ^ jnp.minimum(seq + 1, spans - 1)

    def place_of(bits):
        return jnp.where(bits == 7, 6, jnp.where(bits == 3, 4, 0))

    scalars = jnp.stack(
        [
            seq, lengths[0], place_of(before), place_of(after),
            seq > 0, seq < spans - 1, row,
            jnp.where(after == 7, 7, jnp.where(after == 3, 5, 4)),
            *[seq ^ k for k in token_order], *[0] * 9,
            *[seq ^ k for k in grad_order], *[0] * 9,
            *[token_order.index(k) for k in grad_order],
        ]
    ).astype(jnp.int32)
    own, cot = tokens[0], cotangent[0]
    gain_in, gain_mid = attn_gain[None], mlp_gain[None]

    tags = buckets[0]
    own = packed(scalars, own, tags)
    mate, near, far_a, far_b = (swap(own, "seq", bits) for bits in (1, 2, 4, 6))
    early, qkv, phi_q, phi_k, expo, blend, num, den, proj = own_forward(
        scalars, own, gain_in, qkv_weight, feature_proj, cot, tags
    )
    mate, near, early = lax.optimization_barrier((mate, near, early))
    some = others_forward(
        scalars, 0, jnp.stack([mate, near]), gain_in, qkv_weight, proj
    )
    far_a, far_b, some, early = lax.optimization_barrier((far_a, far_b, some, early))
    far = swap(jnp.stack([near, far_a, far_b]), "seq", 1)
    early_parts = [swap(early, "dp", k) for k in (1, 2, 3)]
    tags_all, u, v, phi, sums, norms = others_forward(
        scalars, 2, jnp.concatenate([jnp.stack([far_a, far_b]), far], 0), gain_in, qkv_weight, proj, some
    )
    others = (tags_all, u, v, phi)
    results = middle(
        scalars, own, qkv, phi_q, sums, norms, num, den, tags, others, gain_mid, out_weight,
        up_weight, down_weight, cot,
    )
    results, early_parts = lax.optimization_barrier((results, early_parts))
    early = (early, *early_parts)
    layer_out, dmid, dn_low, dnum, dden, expo_e, blend_e, gmlp = results[4:]
    pays = exchange(scalars, *results[0:4], dmid)
    pay_1, pay_2 = pays[0:4], pays[4:8]
    dn_far = [swap(dn_low, "seq", bits) for bits in (2, 4, 6)]
    parts_1 = [pay_1[0], swap(pay_1[1], "dp", 1), swap(pay_1[2], "dp", 2)]
    dq, dk, dv, dphi = own_back(
        scalars, tags, qkv, phi_q, phi_k, proj, expo, blend, dnum, dden, sums, norms, others,
        expo_e, blend_e,
    )
    parts_1, last_1, dk = lax.optimization_barrier((parts_1, pay_1[3], dk))
    parts_1.append(swap(last_1, "dp", 3))
    dn_half = jnp.stack([dn_low, *dn_far])
    dn_pieces = jnp.concatenate([dn_half, swap(dn_half, "seq", 1)], 0)
    parts_1, pay_2 = lax.optimization_barrier((parts_1, pay_2))
    parts_2 = [pay_2[0]] + [swap(pay_2[k], "dp", k) for k in (1, 2, 3)]
    keep, send = weights(first_kernel, scalars, (*parts_1, *early), ROWS_1, D, [(D, D), (384, 384)])
    total_1 = keep + swap(send, "seq", 1).astype(F32)
    total_1, dn_pieces = lax.optimization_barrier((total_1, dn_pieces))
    *pay_3, grad_tokens = last(
        scalars, dn_pieces, others, own, tags, qkv, phi_k, proj, dq, dk, dv, dphi, dmid, gain_in,
        qkv_weight, gmlp,
    )
    pay_3, parts_2 = lax.optimization_barrier((pay_3, parts_2))
    share_1 = reduce_spans(total_1[0:2], total_1[2:4].astype(BF), (2, 4))
    parts_3 = [pay_3[0]] + [swap(pay_3[k], "dp", k) for k in (1, 2, 3)]
    keep, send = weights(second_kernel, scalars, parts_2, ROWS_2, D, [(D, D)])
    total_2 = keep + swap(send, "seq", 1).astype(F32)
    total_2 = total_2[0:2] + swap(total_2[2:4].astype(BF), "seq", 2).astype(F32)
    parts_3, share_1, total_2 = lax.optimization_barrier((parts_3, share_1, total_2))
    share_2 = reduce_spans(total_2[0:1], total_2[1:2].astype(BF), (4,))
    share_3 = reduce_spans(*weights(third_kernel, scalars, (*parts_3, *early), ROWS_B, WIN, [(D, WIN)]))

    def everywhere(share):
        return [share] + [swap(share, "dp", k) for k in (1, 2, 3)]

    down, out = spread(fill_first, scalars, everywhere(share_1), [(384, D), (96, D)])
    (up,) = spread(fill_second, scalars, everywhere(share_2), [(96, 4 * D)])
    grad_qkv, gains = spread(fill_third, scalars, everywhere(share_3), [(96, 3 * D), (8, WIN)])
    gains = gains[0:4].reshape(2, 2 * WIN)[:, 0:D]
    mine = lax.dynamic_slice_in_dim(gains, seq * 96, 96, 1)
    return (
        layer_out[None], grad_tokens[None], grad_qkv, out, up, down, mine[0], mine[1],
    )


SPARSE_BLOCK = 64


HIGH_PRECISION = lax.Precision.HIGHEST
FLOAT = jnp.float32
HALF = jnp.bfloat16


def from_behind(array, axis, by):
    size = lax.axis_size(axis)
    pairs = [(i, i + by) for i in range(size) if 0 <= i + by < size]
    return lax.ppermute(array, axis, pairs)


def prefix(value, axis, join, neutral, backward):
    count, mine = (lax.axis_size(axis), lax.axis_index(axis))
    pieces = jax.tree.map(lambda part: lax.all_gather(part, axis), value)
    if backward:
        pieces = jax.tree.map(lambda part: part[::-1], pieces)
        mine = count - 1 - mine
    so_far = jax.tree.map(
        lambda part, zero: jnp.full_like(part, 0) + jnp.asarray(zero, part.dtype), value, neutral
    )

    def hop(position, so_far):
        longer = join(so_far, jax.tree.map(lambda part: part[position], pieces))
        return jax.tree.map(lambda new, old: jnp.where(position < mine, new, old), longer, so_far)

    return lax.fori_loop(0, count - 1, hop, so_far)


def shortened(array):

    def short(part):
        return part.astype(jnp.bfloat16) if part.dtype == jnp.float32 else part

    return jax.tree.map(short, array)


def layer_norm(value_rows, gain):
    center = value_rows - jnp.mean(value_rows, -1, keepdims=True)
    spread = jnp.mean(center * center, -1, keepdims=True)
    return center * lax.rsqrt(spread + EPS) * gain


def feature_map(inputs, feature_proj):
    factor = feature_proj.shape[0] ** (-0.25)
    linear = jnp.einsum("rlhd,dm->rlhm", inputs, feature_proj, precision=HIGH_PRECISION) * factor
    square = 0.5 * factor * factor * jnp.sum(inputs * inputs, -1, keepdims=True)
    return jnp.exp(linear - square) * feature_proj.shape[1] ** (-0.5)


def feature_back(inputs, phi_vals, upstream, feature_proj):
    factor = feature_proj.shape[0] ** (-0.25)
    weighted = upstream * phi_vals
    linear = jnp.einsum("rlhm,dm->rlhd", weighted, feature_proj, precision=HIGH_PRECISION) * factor
    return linear - factor * factor * inputs * jnp.sum(weighted, -1, keepdims=True)


def add_pair(first, second):
    return (first[0] + second[0], first[1] + second[1])


def attention_parts(query, keys, tag_window, lengths, feature_proj, first_pos):
    tok_count = query.shape[1]
    key_count = keys.shape[1]
    query_pos = first_pos + jnp.arange(tok_count, dtype=jnp.int32)
    key_pos = first_pos - SPARSE_BLOCK + jnp.arange(key_count, dtype=jnp.int32)
    query_ok = query_pos[None, :] < lengths[:, None]
    key_ok = (key_pos[None, :] >= 0) & (key_pos[None, :] < lengths[:, None])
    own_flag = jnp.arange(key_count) >= SPARSE_BLOCK
    causal = key_pos[None, :] <= query_pos[:, None]
    near_block = key_pos[None, :] // SPARSE_BLOCK >= query_pos[:, None] // SPARSE_BLOCK - 1
    allowed = causal[None, None] & key_ok[:, None, None, :]
    matched = (
        (tag_window[:, :, SPARSE_BLOCK:, None] == tag_window[:, :, None, :])
        & allowed
        & near_block[None, None]
    )
    phi_query = feature_map(query.astype(FLOAT), feature_proj)
    phi_keys = feature_map(keys.astype(FLOAT), feature_proj)
    query_features = phi_query.astype(HALF)
    feat_keys = phi_keys.astype(HALF)
    scores = jnp.einsum(
        "rthd,rjhd->rhtj", query, keys, preferred_element_type=FLOAT
    ) * feature_proj.shape[0] ** (-0.5)
    exponent = jnp.exp(scores)
    approx = jnp.einsum("rthm,rjhm->rhtj", query_features, feat_keys, preferred_element_type=FLOAT)
    blended = jnp.where(
        matched,
        jnp.where(own_flag, exponent, exponent - approx),
        jnp.where(own_flag & allowed, approx, 0.0),
    )
    return (
        query_ok,
        key_ok,
        own_flag,
        allowed,
        matched,
        phi_query,
        phi_keys,
        query_features,
        feat_keys,
        exponent,
        blended,
    )


def per_device(
    tokens,
    lengths,
    buckets,
    feature_proj,
    attn_gain,
    qkv_weight,
    out_weight,
    mlp_gain,
    up_weight,
    down_weight,
    cotangent,
):
    row_count, tok_count, model_width = tokens.shape
    head_count = buckets.shape[1]
    head_size = model_width // head_count
    resid = tokens.astype(FLOAT)
    normed_in = layer_norm(resid, attn_gain).astype(HALF)
    projected = jnp.dot(normed_in, qkv_weight, preferred_element_type=FLOAT).astype(HALF)
    shaped = projected.reshape(row_count, tok_count, 3, head_count, head_size)
    query = shaped[:, :, 0]
    own_keys = shaped[:, :, 1]
    own_values = shaped[:, :, 2]
    tags = buckets.astype(HALF)
    edge_keys, edge_values, edge_tags = from_behind(
        (own_keys[:, -SPARSE_BLOCK:], own_values[:, -SPARSE_BLOCK:], tags[:, :, -SPARSE_BLOCK:]),
        "seq",
        1,
    )
    keys = jnp.concatenate([edge_keys, own_keys], 1)
    value_rows = jnp.concatenate([edge_values, own_values], 1)
    tag_window = jnp.concatenate([edge_tags, tags], 2)
    first_pos = lax.axis_index("seq") * tok_count
    (
        query_ok,
        key_ok,
        own_flag,
        allowed,
        matched,
        phi_query,
        phi_keys,
        query_features,
        feat_keys,
        exponent,
        blended,
    ) = attention_parts(query, keys, tag_window, lengths, feature_proj, first_pos)
    retained_features = jnp.where(
        key_ok[:, SPARSE_BLOCK:, None, None],
        feat_keys[:, SPARSE_BLOCK:],
        jnp.zeros_like(feat_keys[:, SPARSE_BLOCK:]),
    )
    sum_add = jnp.einsum(
        "rthm,rthd->rhmd", retained_features, own_values, preferred_element_type=FLOAT
    )
    norm_add = jnp.sum(retained_features.astype(FLOAT), 1)
    zero_sums = jnp.zeros_like(sum_add)
    zero_norms = jnp.zeros_like(norm_add)
    running_feature_sums, carry_norms = prefix(
        (sum_add, norm_add), "seq", add_pair, (zero_sums, zero_norms), False
    )
    feat_query_f = query_features.astype(FLOAT)
    blended_low = blended.astype(HALF)
    attention_numerator = jnp.einsum(
        "rthm,rhmd->rthd", feat_query_f, running_feature_sums, precision=HIGH_PRECISION
    )
    attention_numerator = attention_numerator + jnp.einsum(
        "rhtj,rjhd->rthd", blended_low, value_rows, preferred_element_type=FLOAT
    )
    denominator = jnp.einsum(
        "rthm,rhm->rth", feat_query_f, carry_norms, precision=HIGH_PRECISION
    ) + jnp.sum(blended, -1).transpose(0, 2, 1)
    den_safe = jnp.where(query_ok[..., None], denominator, 1.0)
    attended = jnp.where(query_ok[..., None, None], attention_numerator / den_safe[..., None], 0.0)
    attended_low = attended.reshape(row_count, tok_count, model_width).astype(HALF)
    mid_resid = resid + jnp.dot(attended_low, out_weight, preferred_element_type=FLOAT)
    normed_mid = layer_norm(mid_resid, mlp_gain).astype(HALF)
    pre_act = jnp.dot(normed_mid, up_weight, preferred_element_type=FLOAT)
    hidden = jax.nn.gelu(pre_act, approximate=True).astype(HALF)
    layer_out = (mid_resid + jnp.dot(hidden, down_weight, preferred_element_type=FLOAT)).astype(
        HALF
    )
    upstream = cotangent.astype(FLOAT)
    grad_down = jnp.einsum("rtf,rtd->fd", hidden, cotangent, preferred_element_type=FLOAT)
    grad_hidden = jnp.einsum("rtd,fd->rtf", cotangent, down_weight, preferred_element_type=FLOAT)
    gelu_vals, gelu_pull = jax.vjp(lambda inner: jax.nn.gelu(inner, approximate=True), pre_act)
    grad_pre = gelu_pull(grad_hidden)[0].astype(HALF)
    grad_up = jnp.einsum("rtd,rtf->df", normed_mid, grad_pre, preferred_element_type=FLOAT)
    grad_normed_mid = jnp.einsum("rtf,df->rtd", grad_pre, up_weight, preferred_element_type=FLOAT)
    mid_vals, mid_pull = jax.vjp(layer_norm, mid_resid, mlp_gain)
    grad_mid_part, grad_mlp_gain = mid_pull(grad_normed_mid)
    grad_mid = upstream + grad_mid_part
    grad_out = jnp.einsum(
        "rtd,rte->de", attended_low.astype(FLOAT), grad_mid, precision=HIGH_PRECISION
    )
    grad_att = jnp.einsum(
        "rte,de->rtd", grad_mid, out_weight.astype(FLOAT), precision=HIGH_PRECISION
    ).astype(HALF)
    grad_att = grad_att.astype(FLOAT).reshape(row_count, tok_count, head_count, head_size)
    grad_numer = jnp.where(query_ok[..., None, None], grad_att / den_safe[..., None], 0.0)
    grad_denom = -jnp.sum(grad_numer * attention_numerator, -1) / den_safe
    grad_feat_query = (
        jnp.einsum("rthd,rhmd->rthm", grad_numer, running_feature_sums, precision=HIGH_PRECISION)
        + grad_denom[..., None] * carry_norms[:, None]
    )
    grad_carry_sums = jnp.einsum(
        "rthm,rthd->rhmd", feat_query_f, grad_numer, precision=HIGH_PRECISION
    )
    grad_carry_norms = jnp.einsum(
        "rthm,rth->rhm", feat_query_f, grad_denom, precision=HIGH_PRECISION
    )
    later_sums, later_norms = prefix(
        (grad_carry_sums, grad_carry_norms), "seq", add_pair, (zero_sums, zero_norms), True
    )
    grad_blend = (
        jnp.einsum(
            "rthd,rjhd->rhtj", grad_numer, value_rows.astype(FLOAT), precision=HIGH_PRECISION
        )
        + grad_denom.transpose(0, 2, 1)[..., None]
    )
    grad_values = jnp.einsum(
        "rhtj,rthd->rjhd", blended_low.astype(FLOAT), grad_numer, precision=HIGH_PRECISION
    )
    grad_expo = jnp.where(matched, grad_blend, 0.0)
    grad_approx = jnp.where(
        matched,
        jnp.where(own_flag, 0.0, -grad_blend),
        jnp.where(own_flag & allowed, grad_blend, 0.0),
    )
    grad_scores = grad_expo * exponent * head_size ** (-0.5)
    grad_query = jnp.einsum(
        "rhtj,rjhd->rthd", grad_scores, keys.astype(FLOAT), precision=HIGH_PRECISION
    )
    grad_keys = jnp.einsum(
        "rhtj,rthd->rjhd", grad_scores, query.astype(FLOAT), precision=HIGH_PRECISION
    )
    grad_feat_query = grad_feat_query + jnp.einsum(
        "rhtj,rjhm->rthm", grad_approx, feat_keys.astype(FLOAT), precision=HIGH_PRECISION
    )
    grad_feat_keys = jnp.einsum(
        "rhtj,rthm->rjhm", grad_approx, feat_query_f, precision=HIGH_PRECISION
    )
    own_mask = key_ok[:, SPARSE_BLOCK:, None, None]
    carry_feat = (
        jnp.einsum(
            "rthd,rhmd->rthm", own_values.astype(FLOAT), later_sums, precision=HIGH_PRECISION
        )
        + later_norms[:, None]
    )
    carry_vals = jnp.einsum(
        "rthm,rhmd->rthd",
        feat_keys[:, SPARSE_BLOCK:].astype(FLOAT),
        later_sums,
        precision=HIGH_PRECISION,
    )
    grad_feat_keys = jnp.concatenate(
        [
            grad_feat_keys[:, :SPARSE_BLOCK],
            grad_feat_keys[:, SPARSE_BLOCK:] + jnp.where(own_mask, carry_feat, 0.0),
        ],
        1,
    )
    grad_values = jnp.concatenate(
        [
            grad_values[:, :SPARSE_BLOCK],
            grad_values[:, SPARSE_BLOCK:] + jnp.where(own_mask, carry_vals, 0.0),
        ],
        1,
    )
    grad_query = grad_query + feature_back(
        query.astype(FLOAT), phi_query, grad_feat_query, feature_proj
    )
    grad_keys = grad_keys + feature_back(keys.astype(FLOAT), phi_keys, grad_feat_keys, feature_proj)
    back_keys, back_values = from_behind(
        (shortened(grad_keys[:, :SPARSE_BLOCK]), shortened(grad_values[:, :SPARSE_BLOCK])),
        "seq",
        -1,
    )
    own_grad_keys = grad_keys[:, SPARSE_BLOCK:]
    own_grad_values = grad_values[:, SPARSE_BLOCK:]
    own_grad_keys = jnp.concatenate(
        [
            own_grad_keys[:, : tok_count - SPARSE_BLOCK],
            own_grad_keys[:, tok_count - SPARSE_BLOCK :] + back_keys,
        ],
        1,
    )
    own_grad_values = jnp.concatenate(
        [
            own_grad_values[:, : tok_count - SPARSE_BLOCK],
            own_grad_values[:, tok_count - SPARSE_BLOCK :] + back_values,
        ],
        1,
    )
    grad_proj = (
        jnp.stack([grad_query, own_grad_keys, own_grad_values], 2)
        .reshape(row_count, tok_count, 3 * model_width)
        .astype(HALF)
    )
    grad_qkv = jnp.einsum("rtd,rte->de", normed_in, grad_proj, preferred_element_type=FLOAT)
    grad_normed_in = jnp.einsum("rte,de->rtd", grad_proj, qkv_weight, preferred_element_type=FLOAT)
    in_vals, in_pull = jax.vjp(layer_norm, resid, attn_gain)
    grad_in_part, grad_attn_gain = in_pull(grad_normed_in)
    grad_tokens = grad_mid + grad_in_part
    shares = (
        lax.psum_scatter(grad_qkv, "seq", scatter_dimension=0, tiled=True),
        lax.psum_scatter(grad_out, "seq", scatter_dimension=0, tiled=True),
        lax.psum_scatter(grad_up, "seq", scatter_dimension=0, tiled=True),
        lax.psum_scatter(grad_down, "seq", scatter_dimension=0, tiled=True),
        lax.psum_scatter(grad_attn_gain, "seq", scatter_dimension=0, tiled=True),
        lax.psum_scatter(grad_mlp_gain, "seq", scatter_dimension=0, tiled=True),
    )
    totals = lax.psum((shares[0], shares[1], shares[2], shares[3], shares[4], shares[5]), "dp")
    return (
        layer_out,
        grad_tokens,
        totals[0],
        totals[1],
        totals[2],
        totals[3],
        totals[4],
        totals[5],
    )


def solution(mesh):
    in_specs = (
        P("dp", "seq", None),
        P("dp"),
        P("dp", None, "seq"),
        P(),
        P(),
        P(),
        P(),
        P(),
        P(),
        P(),
        P("dp", "seq", None),
    )
    out_specs = (
        P("dp", "seq", None),
        P("dp", "seq", None),
        P("seq", None),
        P("seq", None),
        P("seq", None),
        P("seq", None),
        P("seq"),
        P("seq"),
    )
    shape = dict(mesh.shape)
    fast = shape == {"dp": 4, "seq": 8}
    return jax.shard_map(
        per_device_fast if fast else per_device, mesh=mesh, in_specs=in_specs, out_specs=out_specs, check_vma=False
    )
```

```python
import functools

import jax
import jax.numpy as jnp
from jax import lax
from jax.experimental import pallas as pl
from jax.experimental.pallas import tpu as pltpu
from jax.sharding import PartitionSpec as P

EPS = 1e-05
F32 = jnp.float32
BF = jnp.bfloat16
T = 128
D = 768
H = 12
HD = 64
M = 256
HM = H * M
PAIRS = H // 2
EDGE = 64
WIN = 640
ROWS_1 = 120
ROWS_2 = 96
ROWS_B = 104
MIB = 1 << 20
AFTER = {'b1': ['d4', 'a2'], 'b2': ['a2', 'a3', 'd4'], 'W2': ['L'], 'p1': ['b1', 'b2', 'b3', 'a1', 'a2', 'a3'], 'p2': ['b1', 'b3', 'd2', 'b2'], 'p3': ['b2', 'd2', 'b1'], 'W3': ['t1'], 'L': ['W1', 'a1', 'a2', 'r1', 'E'], 'h1': ['t2', 'g1', 'g2', 'g3', 's3', 'W3'], 'h2': ['t2', 'g1', 'g2', 'g3', 's3', 'p2', 'W3'], 'h3': ['g2', 'g3', 'W3'], 'W1': ['d4', 'd2'], 't2': ['r3', 'r2', 'b1', 'p3'], 's1': ['W1', 'a1', 'a2', 'OB'], 'g2': ['L', 'W2'], 'i1': ['g3', 't3'], 'i2': ['g3', 't3', 'r3', 't1', 'W3'], 'S3': ['g2', 'g3', 'S2'], 'i3': ['W3'], 'a2': ['E'], 'r2': ['r1'], 'r3': ['b1', 'b2', 'b3'], 'a1': ['E'], 'a3': ['E'], 'late': []}


def nn(a, b):
    return lax.dot_general(a, b, (((1,), (0,)), ((), ())), preferred_element_type=F32)


def nt(a, b):
    return lax.dot_general(a, b, (((1,), (1,)), ((), ())), preferred_element_type=F32)


def tn(a, b):
    return lax.dot_general(a, b, (((0,), (0,)), ((), ())), preferred_element_type=F32)


def split(a):
    high = a.astype(BF)
    return high, (a - high.astype(F32)).astype(BF)


def iota(shape, axis):
    return lax.broadcasted_iota(jnp.int32, shape, axis)


def lanes(*parts):
    return jnp.concatenate(parts, axis=1)


def norm_parts(value):
    center = value - jnp.mean(value, -1, keepdims=True)
    scale = lax.rsqrt(jnp.mean(center * center, -1, keepdims=True) + EPS)
    return center * scale, scale


def norm_back(unit, scale, gain, upstream):
    inner = upstream * gain
    return scale * (
        inner
        - jnp.mean(inner, -1, keepdims=True)
        - unit * jnp.mean(inner * unit, -1, keepdims=True)
    )


def phi_pair(pair, proj):
    return phi_of(pair, nn(lanes(pair, pair), proj))


def phi_of(pair, linear):
    wide = pair.astype(F32)
    square = wide * wide
    first = iota(square.shape, 1) < HD
    out = []
    for half in range(2):
        mine = first if half == 0 else ~first
        total = jnp.sum(jnp.where(mine, square, 0.0), -1, keepdims=True)
        out.append(
            jnp.exp(linear[:, half * M : half * M + M] - total * (0.5 * HD**-0.5)) * M**-0.5
        )
    return out


def phi_back(pair, grads, phis, proj):
    weighted = [grad * phi for grad, phi in zip(grads, phis)]
    joined = lanes(*weighted)
    high, low = split(joined)
    linear = nt(high, proj[:128]) + nt(high, proj[128:]) + nt(low, proj[:128])
    sums = [jnp.sum(part, -1, keepdims=True) for part in weighted]
    first = iota(pair.shape, 1) < HD
    return linear - HD**-0.5 * pair.astype(F32) * jnp.where(first, sums[0], sums[1])


def pick(first, two):
    return jnp.where(first, two[0], two[1])


def masked(first, half, value):
    zero = jnp.zeros_like(value)
    return jnp.where(first, value, zero) if half == 0 else jnp.where(first, zero, value)


def columns_to(acc, head, column):
    return jnp.where(iota(acc.shape, 1) == head, column, acc)


def rounded(value):
    return value.astype(BF)


def call(kernel, scalars, args, in_specs, outs, out_specs, grid, scratch=(), flops=0, size=0, vmem=48, aliases=None):
    return pl.pallas_call(
        kernel,
        out_shape=outs,
        grid_spec=pltpu.PrefetchScalarGridSpec(
            num_scalar_prefetch=1,
            grid=grid,
            in_specs=in_specs,
            out_specs=out_specs,
            scratch_shapes=list(scratch),
        ),
        input_output_aliases=aliases or {},
        compiler_params=pltpu.CompilerParams(vmem_limit_bytes=vmem * MIB),
        cost_estimate=pl.CostEstimate(flops=flops // 1000, bytes_accessed=size // 1000, transcendentals=0),
    )(scalars, *args)


def whole(shape):
    return pl.BlockSpec(memory_space=pltpu.VMEM)


def sds(shape, dtype):
    return jax.ShapeDtypeStruct(shape, dtype)


def projection(feature_proj):
    scaled = feature_proj * HD ** (-0.25)
    high, low = split(scaled)
    none = jnp.zeros((HD, M), BF)
    return jnp.concatenate([lanes(high, none), lanes(none, high), lanes(low, none), lanes(none, low)], 0)


def pack_kernel(sc, x_ref, tag_ref, out_ref, tags_ref):
    out_ref[0:T, :] = x_ref[...]
    rows = [tag_ref[h].astype(F32) for h in range(H)]
    wide = [lanes(*rows[6 * r : 6 * r + 6]) for r in range(2)]
    out_ref[T : T + 8, :] = jnp.concatenate(wide + [jnp.zeros((6, D), F32)], 0).astype(BF)
    tags_ref[...] = jnp.concatenate(rows + [jnp.zeros((4, T), F32)], 0)


def packed(scalars, own, tags):
    outs = (sds((T + 8, D), BF), sds((16, T), F32))
    return call(
        pack_kernel, scalars, (own, tags), [whole(own.shape), whole(tags.shape)], outs,
        [whole(o.shape) for o in outs], (1,), vmem=2,
    )


def tag_pair(ref):
    return ref[...], ref[...].T


def own_kernel(
    sc, x_ref, gain_ref, w_ref, feature_ref, g_ref, tag_ref,
    pay_ref, qkv_ref, phiq_ref, phik_ref, expo_ref, blend_ref, num_ref, den_ref, proj_ref,
):
    unit, _ = norm_parts(x_ref[0:T, :].astype(F32))
    normed = unit * gain_ref[...]
    low = normed.astype(BF)
    pay_ref[0:D, :] = normed.T.astype(BF)
    for t in range(6):
        pay_ref[D + 128 * t : D + 128 * t + 128, :] = g_ref[:, 128 * t : 128 * t + 128]
    qkv_ref[...] = nn(low, w_ref[...]).astype(BF)
    rows, cols = tag_pair(tag_ref)
    first = iota((T, 128), 1) < HD
    query_at, key_at = iota((T, T), 0), iota((T, T), 1)
    allowed = (key_at <= query_at) & (key_at + sc[0] * T < sc[1])
    dens = jnp.zeros((T, 128), F32)
    proj = projection(feature_ref[...])
    proj_ref[...] = proj
    for p in range(PAIRS):
        at = slice(128 * p, 128 * p + 128)
        query, key, value = (
            qkv_ref[:, part * D + 128 * p : part * D + 128 * p + 128] for part in range(3)
        )
        phi_q, phi_k = phi_pair(query, proj), phi_pair(key, proj)
        nums = []
        for half in range(2):
            h = 2 * p + half
            phiq_ref[:, M * h : M * h + M] = phi_q[half]
            phik_ref[:, M * h : M * h + M] = phi_k[half]
            expo = jnp.exp(nt(masked(first, half, query), key) * HD**-0.5)
            approx = nt(phi_q[half].astype(BF), phi_k[half].astype(BF))
            matched = allowed & (cols[:, h : h + 1] == rows[h : h + 1, :])
            blend = jnp.where(matched, expo, jnp.where(allowed, approx, 0.0))
            expo_ref[h] = jnp.where(matched, expo, 0.0)
            blend_ref[h] = blend.astype(BF)
            nums.append(nn(blend.astype(BF), value))
            dens = columns_to(dens, h, jnp.sum(blend, -1, keepdims=True))
        num_ref[:, at] = pick(first, nums)
    den_ref[...] = dens


def own_forward(scalars, own, gain, qkv_weight, feature_proj, cotangent, tags):
    outs = (
        sds((2 * D, 128), BF), sds((T, 3 * D), BF), sds((T, HM), F32), sds((T, HM), F32),
        sds((H, T, T), F32), sds((H, T, T), BF), sds((T, D), F32), sds((T, 128), F32),
        sds((2 * 128, 2 * M), BF),
    )
    args = (own, gain, qkv_weight, feature_proj, cotangent, tags)
    return call(
        own_kernel, scalars, args, [whole(a.shape) for a in args], outs,
        [whole(o.shape) for o in outs], (1,), vmem=6, flops=2_000_000_000, size=9_000_000,
    )


def others_kernel(begin, sc, x_ref, gain_ref, w_ref, proj_ref, *refs):
    tags_ref, u_ref, v_ref, phi_ref, sums_ref, norms_ref = refs[-6:]
    slot = pl.program_id(0)
    at = begin + slot
    span = sc[8 + at]

    @pl.when(slot == 0)
    def _():
        if begin:
            sums_ref[...], norms_ref[...] = refs[4][...], refs[5][...]
        else:
            sums_ref[...] = jnp.zeros_like(sums_ref)
            norms_ref[...] = jnp.zeros_like(norms_ref)

    unit, _ = norm_parts(x_ref[slot, 0:T, :].astype(F32))
    wide = x_ref[slot, T : T + 8, :].astype(F32)
    rows = [wide[h // 6 : h // 6 + 1, 128 * (h % 6) : 128 * (h % 6) + 128] for h in range(H)]
    tags_ref[at] = jnp.concatenate(rows + [jnp.zeros((4, 128), F32)], 0)
    low = (unit * gain_ref[...]).astype(BF)
    earlier = span < sc[0]
    offset = pl.multiple_of(jnp.where(earlier, D, 0), D)
    u_ref[at] = nn(low, w_ref[:, pl.ds(offset, D)]).astype(BF)
    pairs = [u_ref[at, :, 128 * p : 128 * p + 128] for p in range(PAIRS)]
    linear = nn(jnp.concatenate([lanes(a, a) for a in pairs], 0), proj_ref[...])
    for p in range(PAIRS):
        phis = phi_of(pairs[p], linear[T * p : T * p + T])
        for half in range(2):
            h = 2 * p + half
            phi_ref[at, :, M * h : M * h + M] = phis[half].astype(BF)

    @pl.when(earlier)
    def _():
        value = nn(low, w_ref[:, 2 * D : 3 * D])
        v_ref[at] = value.astype(BF)
        valid = iota((T, 1), 0) + span * T < sc[1]
        turned = jnp.where(valid, value, 0.0).T.astype(BF)
        ones = jnp.where(iota((16, T), 1) + span * T < sc[1], 1.0, 0.0).astype(BF)
        for h in range(H):
            hm = slice(M * h, M * h + M)
            total = nn(jnp.concatenate([turned[HD * h : HD * h + HD, :], ones], 0), phi_ref[at, :, hm])
            sums_ref[HD * h : HD * h + HD, :] += total[0:HD]
            norms_ref[:, hm] += total[HD : HD + 8]

    @pl.when(~earlier)
    def _():
        v_ref[at] = jnp.zeros((T, D), BF)


def others_forward(scalars, begin, pieces, gain, qkv_weight, proj, so_far=()):
    count, spans = pieces.shape[0], 7
    outs = (
        sds((spans, 16, T), F32), sds((spans, T, D), BF), sds((spans, T, D), BF), sds((spans, T, HM), BF),
        sds((D, M), F32), sds((8, HM), F32),
    )
    args = (pieces, gain, qkv_weight, proj, *so_far)
    return call(
        functools.partial(others_kernel, begin), scalars, args, [whole(a.shape) for a in args], outs,
        [whole(o.shape) for o in outs], (count,), vmem=8, flops=0, size=0,
        aliases={5: 0, 6: 1, 7: 2, 8: 3} if so_far else {},
    )


def rows_of(wide, begin):
    rows = [wide[begin + h // 6 : begin + h // 6 + 1, 128 * (h % 6) : 128 * (h % 6) + 128] for h in range(H)]
    return jnp.concatenate(rows + [jnp.zeros((4, 128), F32)], 0)


def middle_kernel(
    sc, x_ref, qkv_ref, phiq_ref, sums_ref, norms_ref, numl_ref, denl_ref, tags_ref,
    tags_prev, up_prev, vp_prev, phi_prev, gain_ref, wo_ref, wup_ref, wdown_ref, g_ref,
    hid_ref, pre_ref, nm_ref, att_ref, out_ref, dmid_ref, dn_low_ref, dn_ref, dd_ref, expo_ref, blend_ref, gain_out,
    mid_s, nm_s, acc_s, dnm_s, num_s, den_s,
):
    step, prev_at = pl.program_id(0), sc[2]
    first = iota((T, 128), 1) < HD
    valid = iota((T, 1), 0) + sc[0] * T < sc[1]

    @pl.when(step == 0)
    def _():
        _, own = tag_pair(tags_ref)
        prev = tags_prev[prev_at]
        prev_tag = [prev[h : h + 1, EDGE:T] for h in range(H)]
        edge_first = iota((EDGE, 128), 1) < HD
        edge_ok = (sc[4] > 0) & (iota((EDGE, EDGE), 1) + (sc[0] * T - EDGE) < sc[1])
        dens = denl_ref[...]
        zeros = jnp.zeros((EDGE, 128), F32)
        for p in range(PAIRS):
            at = slice(128 * p, 128 * p + 128)
            high, lowp = split(sums_ref[at, :])
            query = qkv_ref[0:EDGE, at]
            key, value = up_prev[prev_at, EDGE:T, at], vp_prev[prev_at, EDGE:T, at]
            nums = []
            for half in range(2):
                h = 2 * p + half
                hm = slice(M * h, M * h + M)
                phi_q = phiq_ref[:, hm].astype(BF)
                total = nt(phi_q, high) + nt(phi_q, lowp)
                den = jnp.sum(phi_q.astype(F32) * norms_ref[0:1, hm], -1, keepdims=True)
                expo = jnp.exp(nt(masked(edge_first, half, query), key) * HD**-0.5)
                approx = nt(phi_q[0:EDGE], phi_prev[prev_at, EDGE:T, hm])
                matched = edge_ok & (own[0:EDGE, h : h + 1] == prev_tag[h])
                blend = jnp.where(matched, expo - approx, 0.0)
                expo_ref[h] = jnp.where(matched, expo, 0.0)
                blend_ref[h] = blend.astype(BF)
                total = total + jnp.concatenate([nn(blend.astype(BF), value), zeros], 0)
                den = den + jnp.concatenate(
                    [jnp.sum(blend, -1, keepdims=True), jnp.zeros((EDGE, 1), F32)], 0
                )
                nums.append(total)
                dens = jnp.where(iota(dens.shape, 1) == h, dens + den, dens)
            num_s[:, at] = numl_ref[:, at] + pick(first, nums)
        dens = jnp.where(valid, dens, 1.0)
        den_s[...] = dens
        for p in range(PAIRS):
            at = slice(128 * p, 128 * p + 128)
            den = jnp.where(first, dens[:, 2 * p : 2 * p + 1], dens[:, 2 * p + 1 : 2 * p + 2])
            mid_s[:, at] = jnp.where(valid, num_s[:, at] / den, 0.0)
        attended = mid_s[...].astype(BF)
        att_ref[...] = attended
        mid = x_ref[0:T, :].astype(F32) + nn(attended, wo_ref[...])
        mid_s[...] = mid
        unit, _ = norm_parts(mid)
        normed = unit * gain_ref[...]
        nm_s[...] = normed.astype(BF)
        nm_ref[...] = normed.astype(BF)
        acc_s[...] = jnp.zeros_like(acc_s)
        dnm_s[...] = jnp.zeros_like(dnm_s)

    pre = nn(nm_s[...], wup_ref[...])
    grad_hidden = nt(g_ref[...], wdown_ref[...])
    root = (2.0 / jnp.pi) ** 0.5
    inner = root * (pre + 0.044715 * (pre * pre * pre))
    tanh = jnp.tanh(inner)
    half_up = 0.5 * (1.0 + tanh)
    hidden = pre * half_up
    slope = half_up + 0.5 * pre * (1.0 - tanh * tanh) * (root * (1.0 + 3 * 0.044715 * (pre * pre)))
    grad_pre = (grad_hidden * slope).astype(BF)
    hidden_low = hidden.astype(BF)
    acc_s[...] += nn(hidden_low, wdown_ref[...])
    dnm_s[...] += nt(grad_pre, wup_ref[...])
    cols = pl.ds(pl.multiple_of(D * step, D), D)
    hid_ref[:, cols] = hidden_low
    pre_ref[:, cols] = grad_pre

    @pl.when(step == 3)
    def _():
        mid = mid_s[...]
        out_ref[...] = (mid + acc_s[...]).astype(BF)
        unit, scale = norm_parts(mid)
        grad = dnm_s[...]
        gain_out[...] = jnp.broadcast_to(jnp.sum(grad * unit, 0, keepdims=True), (8, D))
        dmid = g_ref[...].astype(F32) + norm_back(unit, scale, gain_ref[...], grad)
        dmid_ref[...] = dmid
        high, low = split(dmid)
        datt = (nt(high, wo_ref[...]) + nt(low, wo_ref[...])).astype(BF).astype(F32)
        dens = den_s[...]
        ddens = jnp.zeros((T, 128), F32)
        for p in range(PAIRS):
            at = slice(128 * p, 128 * p + 128)
            den = jnp.where(first, dens[:, 2 * p : 2 * p + 1], dens[:, 2 * p + 1 : 2 * p + 2])
            dnum = jnp.where(valid, datt[:, at] / den, 0.0)
            dn_ref[:, at] = dnum
            dn_low_ref[0:T, at] = dnum.astype(BF)
            prod = dnum * num_s[:, at]
            for half in range(2):
                h = 2 * p + half
                total = jnp.sum(masked(first, half, prod), -1, keepdims=True)
                ddens = columns_to(ddens, h, -total / dens[:, h : h + 1])
        dd_ref[...] = ddens
        ends, tags = ddens.T, tag_pair(tags_ref)[0]
        wide = [lanes(*[a[h : h + 1, :] for h in range(b, b + 6)]) for a in (ends, tags) for b in (0, 6)]
        dn_low_ref[T : T + 8, :] = jnp.concatenate(wide + [jnp.zeros((4, D), F32)], 0).astype(BF)


def middle(scalars, own, qkv, phi_q, sums, norms, num, den, tags, others, gain, wo, wup, wdown, cot):
    tags_all, u, v, phi = others
    outs = (
        sds((T, 4 * D), BF), sds((T, 4 * D), BF), sds((T, D), BF), sds((T, D), BF),
        sds((T, D), BF), sds((T, D), F32), sds((T + 8, D), BF),
        sds((T, D), F32), sds((T, 128), F32), sds((H, EDGE, EDGE), F32), sds((H, EDGE, EDGE), BF),
        sds((8, D), F32),
    )
    args = (own, qkv, phi_q, sums, norms, num, den, tags, tags_all, u, v, phi, gain, wo, wup, wdown, cot)
    specs = [whole(a.shape) for a in args[:14]] + [
        pl.BlockSpec((D, D), lambda i, sc: (0, i)), pl.BlockSpec((D, D), lambda i, sc: (i, 0)), whole(cot.shape),
    ]
    scratch = [
        pltpu.VMEM((T, D), F32), pltpu.VMEM((T, D), BF), pltpu.VMEM((T, D), F32),
        pltpu.VMEM((T, D), F32), pltpu.VMEM((T, D), F32), pltpu.VMEM((T, 128), F32),
    ]
    return call(
        middle_kernel, scalars, args, specs, outs,
        [whole(o.shape) for o in outs], (4,), scratch,
        vmem=12, flops=3_500_000_000, size=20_000_000,
    )


def exchange_kernel(sc, hid_ref, pre_ref, nm_ref, att_ref, dmid_ref, *refs):
    first_pay, second_pay, turn_s = refs[0:4], refs[4:8], refs[8]
    me = sc[6]
    for b in range(4):
        turn_s[D * b : D * b + D, :] = hid_ref[:, D * b : D * b + D].astype(F32).T.astype(BF)
    turned_nm = nm_ref[...].astype(F32).T.astype(BF)
    turned_att = att_ref[...].astype(F32).T.astype(BF)
    dmid = dmid_ref[...].astype(BF)
    for k in range(4):
        mate = me ^ k
        for s in range(8):
            begin = pl.multiple_of(384 * s + 96 * mate, 96)
            first_pay[k][96 * s : 96 * s + 96, :] = turn_s[pl.ds(begin, 96), :]
            first_pay[k][768 + 48 * s : 768 + 48 * s + 48, :] = jnp.where(
                mate >= 2, turned_att[96 * s + 48 : 96 * s + 96, :], turned_att[96 * s : 96 * s + 48, :]
            )
        for t in range(3):
            first_pay[k][1152 + 128 * t : 1152 + 128 * t + 128, :] = jnp.where(
                (mate & 1) > 0, dmid[:, 384 + 128 * t : 512 + 128 * t], dmid[:, 128 * t : 128 * t + 128]
            )
        second_pay[k][0:D, :] = turned_nm
        for t in range(6):
            begin = pl.multiple_of(D * mate + 128 * t, 128)
            second_pay[k][D + 128 * t : D + 128 * t + 128, :] = pre_ref[:, pl.ds(begin, 128)]


def exchange(scalars, *args):
    outs = tuple([sds((2 * D, 128), BF)] * 8)
    return call(
        exchange_kernel, scalars, args, [whole(a.shape) for a in args], outs, [whole(o.shape) for o in outs],
        (1,), [pltpu.VMEM((4 * D, T), BF)], vmem=8,
    )


def own_back_kernel(
    sc, tags_ref, qkv_ref, phiq_ref, phik_ref, proj_ref, expo_ref, blend_ref, dn_ref, dd_ref,
    sums_ref, norms_ref, tags_prev, up_prev, vp_prev, phi_prev, expo_e, blend_e,
    dq_ref, dk_ref, dv_ref, dphi_ref,
):
    prev_at = sc[2]
    rows, cols = tag_pair(tags_ref)
    first = iota((T, 128), 1) < HD
    query_at, key_at = iota((T, T), 0), iota((T, T), 1)
    allowed = (key_at <= query_at) & (key_at + sc[0] * T < sc[1])
    prev_tag = tags_prev[prev_at]
    edge_first = iota((EDGE, 128), 1) < HD
    edge_ok = (sc[4] > 0) & (iota((EDGE, EDGE), 1) + (sc[0] * T - EDGE) < sc[1])
    proj = proj_ref[...]
    for p in range(PAIRS):
        at = slice(128 * p, 128 * p + 128)
        query, key, value = (
            qkv_ref[:, part * D + 128 * p : part * D + 128 * p + 128] for part in range(3)
        )
        key_e, value_e = up_prev[prev_at, EDGE:T, at], vp_prev[prev_at, EDGE:T, at]
        high, low = split(dn_ref[:, at])
        both = lanes(high, low)
        s_high, s_low = split(sums_ref[at, :])
        grads, phis, dqs, dks, dvs = [], [], [], [], []
        for half in range(2):
            h = 2 * p + half
            hm = slice(M * h, M * h + M)
            dden = dd_ref[:, h : h + 1]
            mine = lanes(masked(first, half, high), masked(first, half, low))
            phi_q, phi_k = phiq_ref[:, hm], phik_ref[:, hm]
            dw = nt(mine, lanes(value, value)) + dden
            matched = cols[:, h : h + 1] == rows[h : h + 1, :]
            ds = (dw * expo_ref[h] * HD**-0.5).astype(BF)
            da = jnp.where(allowed & ~matched, dw, 0.0).astype(BF)
            dq = nn(ds, key)
            dks.append(tn(ds, query))
            dv = tn(blend_ref[h], both)
            dvs.append(dv[:, 0:128] + dv[:, 128:256])
            dphi = nn(da, phi_k.astype(BF)) + dden * norms_ref[0:1, hm]
            dphi = dphi + nn(mine, jnp.concatenate([s_high, s_high], 0))
            dphi = dphi + nn(mine[:, 0:128], s_low)
            dphi_ref[:, hm] = tn(da, phi_q.astype(BF))
            edge = nt(mine[0:EDGE], lanes(value_e, value_e)) + dden[0:EDGE]
            matched_e = edge_ok & (cols[0:EDGE, h : h + 1] == prev_tag[h : h + 1, EDGE:T])
            ds_e = (edge * expo_e[h] * HD**-0.5).astype(BF)
            da_e = jnp.where(matched_e, -edge, 0.0).astype(BF)
            dqs.append(dq + jnp.concatenate([nn(ds_e, key_e), jnp.zeros((EDGE, 128), F32)], 0))
            grads.append(
                dphi + jnp.concatenate([nn(da_e, phi_prev[prev_at, EDGE:T, hm]), jnp.zeros((EDGE, M), F32)], 0)
            )
            phis.append(phi_q)
        dq_ref[:, at] = (pick(first, dqs) + phi_back(query, grads, phis, proj)).astype(BF)
        dk_ref[:, at] = pick(first, dks)
        dv_ref[:, at] = pick(first, dvs)


def own_back(scalars, tags, qkv, phi_q, phi_k, proj, expo, blend, dnum, dden, sums, norms, others, expo_e, blend_e):
    tags_all, u, v, phi = others
    args = (
        tags, qkv, phi_q, phi_k, proj, expo, blend, dnum, dden, sums, norms, tags_all, u, v, phi, expo_e,
        blend_e,
    )
    specs = [whole(a.shape) for a in args]
    outs = (sds((T, D), BF), sds((T, D), F32), sds((T, D), F32), sds((T, HM), F32))
    return call(
        own_back_kernel, scalars, args, specs, outs, [whole(o.shape) for o in outs], (1,),
        vmem=8, flops=3_000_000_000, size=9_000_000,
    )


def last_kernel(
    sc, dn_ref, phi_ref, x_ref, tags_ref, qkv_ref, phik_ref, proj_ref, dq_ref, dk_ref, dv_ref, dphi_ref,
    u_ref, dmid_ref, gain_ref, w_ref, gmlp_ref,
    a0, a1, a2, a3, grad_ref, sums_s, norms_s, dqkv_s,
):
    slot = pl.program_id(0)
    span = sc[24 + slot]

    @pl.when(slot == 0)
    def _():
        sums_s[...] = jnp.zeros_like(sums_s)
        norms_s[...] = jnp.zeros_like(norms_s)

    @pl.when(span > sc[0])
    def _():
        turned = dn_ref[slot + 1, 0:T, :].astype(F32).T.astype(BF)
        ends = rows_of(dn_ref[slot + 1, T : T + 8, :].astype(F32), 0).astype(BF)
        for h in range(H):
            hm = slice(M * h, M * h + M)
            total = nn(
                jnp.concatenate([turned[HD * h : HD * h + HD, :], ends], 0), phi_ref[sc[40 + slot], :, hm]
            )
            sums_s[HD * h : HD * h + HD, :] += total[0:HD]
            norms_s[:, hm] += total[HD : HD + 16]

    @pl.when(slot == pl.num_programs(0) - 1)
    def _():
        me, next_at, dn_at = sc[6], sc[3], sc[7]
        rows = tags_ref[...].astype(F32)
        next_cols = rows_of(dn_ref[dn_at, T : T + 8, :].astype(F32), 2).T
        first = iota((T, 128), 1) < HD
        edge_first = iota((EDGE, 128), 1) < HD
        valid = iota((T, 1), 0) + sc[0] * T < sc[1]
        edge_ok = (sc[5] > 0) & (iota((EDGE, EDGE), 1) + (sc[0] * T + EDGE) < sc[1])
        proj = proj_ref[...]
        ddn = rows_of(dn_ref[dn_at, T : T + 8, :].astype(F32), 0).T[0:EDGE]
        dqkv_s[:, 0:D] = dq_ref[...]
        for p in range(PAIRS):
            at = slice(128 * p, 128 * p + 128)
            key, value = (qkv_ref[:, part * D + 128 * p : part * D + 128 * p + 128] for part in (1, 2))
            high, low = split(sums_s[at, :])
            query_n, dnum_n = u_ref[next_at, 0:EDGE, at], dn_ref[dn_at, 0:EDGE, at]
            grads, phis, dks, dvs = [], [], [], []
            for half in range(2):
                h = 2 * p + half
                hm = slice(M * h, M * h + M)
                phi_k = phik_ref[:, hm]
                phi_kb = phi_k.astype(BF)
                mine = masked(first, half, value)
                carry = nn(mine, high) + nn(mine, low) + norms_s[h : h + 1, hm]
                dv = nt(phi_kb, high) + nt(phi_kb, low)
                q_h, d_h = masked(edge_first, half, query_n), masked(edge_first, half, dnum_n)
                phi_n = phi_ref[next_at, 0:EDGE, hm]
                expo = jnp.exp(nt(q_h, key[EDGE:]) * HD**-0.5)
                approx = nt(phi_n, phi_kb[EDGE:])
                matched = edge_ok & (next_cols[0:EDGE, h : h + 1] == rows[h : h + 1, EDGE:128])
                blend = jnp.where(matched, expo - approx, 0.0).astype(BF)
                dw = nt(d_h, value[EDGE:]) + ddn[:, h : h + 1]
                ds = jnp.where(matched, dw * expo * HD**-0.5, 0.0).astype(BF)
                da = jnp.where(matched, -dw, 0.0).astype(BF)
                none = jnp.zeros((EDGE, 128), F32)
                dks.append(jnp.concatenate([none, tn(ds, query_n)], 0))
                dvs.append(jnp.where(valid, dv, 0.0) + jnp.concatenate([none, tn(blend, dnum_n)], 0))
                grads.append(
                    dphi_ref[:, hm] + jnp.where(valid, carry, 0.0)
                    + jnp.concatenate([jnp.zeros((EDGE, M), F32), tn(da, phi_n)], 0)
                )
                phis.append(phi_k)
            dqkv_s[:, D + 128 * p : D + 128 * p + 128] = (
                dk_ref[:, at] + pick(first, dks) + phi_back(key, grads, phis, proj)
            ).astype(BF)
            dqkv_s[:, 2 * D + 128 * p : 2 * D + 128 * p + 128] = (dv_ref[:, at] + pick(first, dvs)).astype(BF)
        grad = nt(dqkv_s[...], w_ref[...])
        unit, scale = norm_parts(x_ref[0:T, :].astype(F32))
        grad_ref[...] = dmid_ref[...] + norm_back(unit, scale, gain_ref[...], grad)
        attn = jnp.sum(grad * unit, 0, keepdims=True)
        mlp = gmlp_ref[0:1, :]
        row = iota((8, WIN), 0)
        gains = jnp.zeros((8, WIN), F32)
        tail = jnp.zeros((1, 2 * WIN - D), F32)
        for at, part in enumerate((attn, mlp)):
            gains = jnp.where(row == 2 * at, part[:, 0:WIN], gains)
            gains = jnp.where(row == 2 * at + 1, lanes(part[:, WIN:D], tail), gains)
        for k, pay_ref in enumerate((a0, a1, a2, a3)):
            mate = me ^ k
            begin = pl.multiple_of(jnp.where(mate == 0, 0, 128 * (4 * mate + 1)), 128)
            pay_ref[0:T, :] = dqkv_s[:, pl.ds(begin, WIN)]
            pay_ref[T : T + 8, :] = gains.astype(BF)


def last(scalars, dn_pieces, others, own, tags, qkv, phi_k, proj, dq, dk, dv, dphi, dmid, gain, qkv_weight, gmlp):
    _, u, v, phi = others
    count = dn_pieces.shape[0] - 1
    args = (
        dn_pieces, phi, own, tags, qkv, phi_k, proj, dq, dk, dv, dphi, u, dmid, gain, qkv_weight, gmlp,
    )
    specs = [whole(a.shape) for a in args]
    outs = tuple([sds((T + 8, WIN), BF)] * 4) + (sds((T, D), F32),)
    return call(
        last_kernel, scalars, args, specs, outs, [whole(o.shape) for o in outs], (count,),
        [pltpu.VMEM((D, M), F32), pltpu.VMEM((16, HM), F32), pltpu.VMEM((T, 3 * D), BF)],
        vmem=10, flops=3_000_000_000, size=count * 1_000_000 + 10_000_000,
    )


def reverse3(at):
    return ((at & 1) << 2) | (at & 2) | (at >> 2)


def place(sc, chunk_of, keep_ref, send_ref):
    for r in range(8):
        block = reverse3(r) ^ sc[0]
        target = keep_ref.at[r] if r < 4 else send_ref.at[r - 4]
        chunk_of(block, target)


def joined(parts, begin, size):
    return lanes(*[part[begin : begin + size, :] for part in parts])


def tiles(part, begin, count):
    return lanes(*[part[begin + 128 * t : begin + 128 * t + 128, :] for t in range(count)])


def product(lefts, rights):
    first = nn(lanes(lefts[0], lefts[1]), jnp.concatenate(rights[0:2], 0))
    return first + nn(lanes(lefts[2], lefts[3]), jnp.concatenate(rights[2:4], 0))


def first_kernel(sc, p0, p1, p2, p3, e0, e1, e2, e3, keep_ref, send_ref, down_s, out_s):
    parts = (p0, p1, p2, p3)
    cots = [e[D : 2 * D, :] for e in (e0, e1, e2, e3)]
    down_s[...] = product([a[0:768, :] for a in parts], [tiles(a, 0, 6) for a in cots])
    out_s[...] = product([a[768:1152, :] for a in parts], [tiles(a, 1152, 3) for a in parts])

    def chunk(block, target):
        at = pl.multiple_of(96 * block, 96)
        target[0:96, :] = down_s[pl.ds(at, 96), :].astype(target.dtype)
        at = pl.multiple_of(48 * block, 48)
        target[96:120, 0:384] = out_s[pl.ds(at, 24), :].astype(target.dtype)
        at = pl.multiple_of(48 * block + 24, 24)
        target[96:120, 384:768] = out_s[pl.ds(at, 24), :].astype(target.dtype)

    place(sc, chunk, keep_ref, send_ref)


def second_kernel(sc, p0, p1, p2, p3, keep_ref, send_ref, up_s):
    parts = (p0, p1, p2, p3)
    up_s[...] = product([a[0:768, :] for a in parts], [tiles(a, 768, 6) for a in parts])

    def chunk(block, target):
        at = pl.multiple_of(96 * block, 96)
        target[...] = up_s[pl.ds(at, 96), :].astype(target.dtype)

    place(sc, chunk, keep_ref, send_ref)


def third_kernel(sc, p0, p1, p2, p3, e0, e1, e2, e3, keep_ref, send_ref, res_s):
    parts = (p0, p1, p2, p3)
    res_s[...] = product([e[0:D, :] for e in (e0, e1, e2, e3)], [a[0:T, :] for a in parts])
    gains = sum(a[T : T + 8, :].astype(F32) for a in parts)

    def chunk(block, target):
        at = pl.multiple_of(96 * block, 96)
        target[0:96, :] = res_s[pl.ds(at, 96), :].astype(target.dtype)
        target[96:104, :] = gains.astype(target.dtype)

    place(sc, chunk, keep_ref, send_ref)


def weights(kernel, scalars, args, rows, width, scratch):
    outs = (sds((4, rows, width), F32), sds((4, rows, width), BF))
    return call(
        kernel, scalars, args, [whole(a.shape) for a in args], outs, [whole(o.shape) for o in outs], (1,),
        [pltpu.VMEM(shape, F32) for shape in scratch], vmem=8, flops=600_000_000, size=20_000_000_000,
    )


def spread_kernel(fill, sc, *refs):
    for k, part in enumerate(refs[0:4]):
        quarter = sc[6] ^ k
        for j in range(4):
            @pl.when(quarter == j)
            def _():
                fill(j, part, *refs[4:])


def spread(fill, scalars, parts, shapes):
    outs = tuple(sds(shape, F32) for shape in shapes)
    return call(
        functools.partial(spread_kernel, fill), scalars, parts, [whole(a.shape) for a in parts], outs,
        [whole(o.shape) for o in outs], (1,), vmem=4, size=2_000_000,
    )


def fill_first(j, part, down_ref, out_ref):
    down_ref[96 * j : 96 * j + 96, :] = part[0:96, :].astype(F32)
    row, col = 48 * (j >> 1), 384 * (j & 1)
    out_ref[row : row + 24, col : col + 384] = part[96:120, 0:384].astype(F32)
    out_ref[row + 24 : row + 48, col : col + 384] = part[96:120, 384:768].astype(F32)


def fill_second(j, part, up_ref):
    up_ref[:, 768 * j : 768 * j + 768] = part[...].astype(F32)


def fill_third(j, part, qkv_ref, gain_ref):
    skip = 128 if j >= 2 else 0
    begin = 0 if j == 0 else 128 * (4 * j + 1)
    qkv_ref[:, begin + skip : begin + WIN] = part[0:96, skip:WIN].astype(F32)
    if j == 0:
        gain_ref[...] = part[96:104, :].astype(F32)


def swap(array, axis, bits):
    size = lax.axis_size(axis)
    return lax.ppermute(array, axis, [(i, i ^ bits) for i in range(size)])


def reduce_spans(keep, send, steps=(1, 2, 4)):
    for bits in steps:
        total = keep + swap(send, "seq", bits).astype(F32)
        half = total.shape[0] // 2
        if half:
            keep, send = total[:half], total[half:].astype(BF)
    return total[0].astype(BF)


def per_device_fast(
    tokens, lengths, buckets, feature_proj, attn_gain, qkv_weight, out_weight, mlp_gain, up_weight,
    down_weight, cotangent,
):
    seq, row = lax.axis_index("seq"), lax.axis_index("dp")
    spans = lax.axis_size("seq")
    token_order, grad_order = (1, 2, 4, 6, 3, 5, 7), (2, 4, 6, 1, 3, 5, 7)
    before, after = seq ^ jnp.maximum(seq - 1, 0), seq ^ jnp.minimum(seq + 1, spans - 1)

    def place_of(bits):
        return jnp.where(bits == 7, 6, jnp.where(bits == 3, 4, 0))

    scalars = jnp.stack(
        [
            seq, lengths[0], place_of(before), place_of(after),
            seq > 0, seq < spans - 1, row,
            jnp.where(after == 7, 7, jnp.where(after == 3, 5, 4)),
            *[seq ^ k for k in token_order], *[0] * 9,
            *[seq ^ k for k in grad_order], *[0] * 9,
            *[token_order.index(k) for k in grad_order],
        ]
    ).astype(jnp.int32)
    own, cot = tokens[0], cotangent[0]
    gain_in, gain_mid = attn_gain[None], mlp_gain[None]

    own, tags = packed(scalars, own, jnp.transpose(buckets, (1, 0, 2)))
    mate, near, far_a, far_b = (swap(own, "seq", bits) for bits in (1, 2, 4, 6))
    early, qkv, phi_q, phi_k, expo, blend, num, den, proj = own_forward(
        scalars, own, gain_in, qkv_weight, feature_proj, cot, tags
    )
    mate, near, early = lax.optimization_barrier((mate, near, early))
    some = others_forward(
        scalars, 0, jnp.stack([mate, near]), gain_in, qkv_weight, proj
    )
    far_a, far_b, some, early = lax.optimization_barrier((far_a, far_b, some, early))
    far = swap(jnp.stack([near, far_a, far_b]), "seq", 1)
    early_parts = [swap(early, "dp", k) for k in (1, 2, 3)]
    tags_all, u, v, phi, sums, norms = others_forward(
        scalars, 2, jnp.concatenate([jnp.stack([far_a, far_b]), far], 0), gain_in, qkv_weight, proj, some
    )
    others = (tags_all, u, v, phi)
    results = middle(
        scalars, own, qkv, phi_q, sums, norms, num, den, tags, others, gain_mid, out_weight,
        up_weight, down_weight, cot,
    )
    results, early_parts = lax.optimization_barrier((results, early_parts))
    early = (early, *early_parts)
    layer_out, dmid, dn_low, dnum, dden, expo_e, blend_e, gmlp = results[4:]
    made = {}

    def after(node, value):
        needs = [made[n] for n in AFTER.get(node, ()) if n in made]
        return lax.optimization_barrier((value, needs))[0] if needs else value

    def move(node, value, axis, bits):
        made[node] = swap(after(node, value), axis, bits)
        return made[node]

    def run(node, work, value, *rest):
        made[node] = work(after(node, value), *rest)
        return made[node]

    def around(node, four):
        return [four[0]] + [move(node + str(k), four[k], "dp", k) for k in (1, 2, 3)]

    dn_4, dn_6 = (move("d" + str(bits), dn_low, "seq", bits) for bits in (4, 6))
    pays = run("E", lambda a: exchange(scalars, *results[0:3], a, dmid), results[3])
    halves = run(
        "OB",
        lambda a: own_back(
            scalars, tags, qkv, phi_q, phi_k, proj, expo, blend, dnum, a, sums, norms, others, expo_e, blend_e
        ),
        dden,
    )
    parts_1 = around("a", pays[0:4])
    dn_half = jnp.stack([dn_low, move("d2", dn_low, "seq", 2), dn_4, dn_6])
    dn_pieces = jnp.concatenate([dn_half, move("c", dn_half, "seq", 1)], 0)
    parts_2 = around("b", pays[4:8])

    def first_weights():
        return run(
            "W1",
            lambda a: weights(
                first_kernel, scalars, (a, *parts_1[1:], *early), ROWS_1, D, [(D, D), (384, 384)]
            ),
            parts_1[0],
        )

    if "late" not in AFTER:
        keep_1, send_1 = first_weights()
        total_1 = keep_1 + move("r1", send_1, "seq", 1).astype(F32)
    *pay_3, grad_tokens = run(
        "L",
        lambda a: last(
            scalars, dn_pieces, others, own, tags, qkv, phi_k, proj, *halves, dmid, gain_in, qkv_weight, a
        ),
        gmlp,
    )
    if "late" in AFTER:
        keep_1, send_1 = first_weights()
        total_1 = keep_1 + move("r1", send_1, "seq", 1).astype(F32)
    total_1 = total_1[0:2] + move("s1", total_1[2:4].astype(BF), "seq", 2).astype(F32)
    parts_3 = around("p", pay_3)
    share_1 = (total_1[0] + move("t1", total_1[1].astype(BF), "seq", 4).astype(F32)).astype(BF)
    keep_2, send_2 = run(
        "W2", lambda a: weights(second_kernel, scalars, (a, *parts_2[1:]), ROWS_2, D, [(D, D)]), parts_2[0]
    )
    total_2 = keep_2 + move("r2", send_2, "seq", 1).astype(F32)
    total_2 = total_2[0:2] + move("s2", total_2[2:4].astype(BF), "seq", 2).astype(F32)
    keep_3, send_3 = run(
        "W3",
        lambda a: weights(third_kernel, scalars, (a, *parts_3[1:], *early), ROWS_B, WIN, [(D, WIN)]),
        parts_3[0],
    )
    total_3 = keep_3 + move("r3", send_3, "seq", 1).astype(F32)
    share_2 = (total_2[0] + move("t2", total_2[1].astype(BF), "seq", 4).astype(F32)).astype(BF)
    total_3 = total_3[0:2] + move("s3", total_3[2:4].astype(BF), "seq", 2).astype(F32)
    parts_1 = around("g", [share_1] * 4)
    share_3 = (total_3[0] + move("t3", total_3[1].astype(BF), "seq", 4).astype(F32)).astype(BF)
    parts_2 = around("h", [share_2] * 4)
    parts_3 = around("i", [share_3] * 4)
    down, out = run(
        "S1", lambda a: spread(fill_first, scalars, [a, *parts_1[1:]], [(384, D), (96, D)]), parts_1[0]
    )
    (up,) = run("S2", lambda a: spread(fill_second, scalars, [a, *parts_2[1:]], [(96, 4 * D)]), parts_2[0])
    grad_qkv, gains = run(
        "S3", lambda a: spread(fill_third, scalars, [a, *parts_3[1:]], [(96, 3 * D), (8, WIN)]), parts_3[0]
    )
    gains = gains[0:4].reshape(2, 2 * WIN)[:, 0:D]
    mine = lax.dynamic_slice_in_dim(gains, seq * 96, 96, 1)
    return (
        layer_out[None], grad_tokens[None], grad_qkv, out, up, down, mine[0], mine[1],
    )


SPARSE_BLOCK = 64


HIGH_PRECISION = lax.Precision.HIGHEST
FLOAT = jnp.float32
HALF = jnp.bfloat16


def from_behind(array, axis, by):
    size = lax.axis_size(axis)
    pairs = [(i, i + by) for i in range(size) if 0 <= i + by < size]
    return lax.ppermute(array, axis, pairs)


def prefix(value, axis, join, neutral, backward):
    count, mine = (lax.axis_size(axis), lax.axis_index(axis))
    pieces = jax.tree.map(lambda part: lax.all_gather(part, axis), value)
    if backward:
        pieces = jax.tree.map(lambda part: part[::-1], pieces)
        mine = count - 1 - mine
    so_far = jax.tree.map(
        lambda part, zero: jnp.full_like(part, 0) + jnp.asarray(zero, part.dtype), value, neutral
    )

    def hop(position, so_far):
        longer = join(so_far, jax.tree.map(lambda part: part[position], pieces))
        return jax.tree.map(lambda new, old: jnp.where(position < mine, new, old), longer, so_far)

    return lax.fori_loop(0, count - 1, hop, so_far)


def shortened(array):

    def short(part):
        return part.astype(jnp.bfloat16) if part.dtype == jnp.float32 else part

    return jax.tree.map(short, array)


def layer_norm(value_rows, gain):
    center = value_rows - jnp.mean(value_rows, -1, keepdims=True)
    spread = jnp.mean(center * center, -1, keepdims=True)
    return center * lax.rsqrt(spread + EPS) * gain


def feature_map(inputs, feature_proj):
    factor = feature_proj.shape[0] ** (-0.25)
    linear = jnp.einsum("rlhd,dm->rlhm", inputs, feature_proj, precision=HIGH_PRECISION) * factor
    square = 0.5 * factor * factor * jnp.sum(inputs * inputs, -1, keepdims=True)
    return jnp.exp(linear - square) * feature_proj.shape[1] ** (-0.5)


def feature_back(inputs, phi_vals, upstream, feature_proj):
    factor = feature_proj.shape[0] ** (-0.25)
    weighted = upstream * phi_vals
    linear = jnp.einsum("rlhm,dm->rlhd", weighted, feature_proj, precision=HIGH_PRECISION) * factor
    return linear - factor * factor * inputs * jnp.sum(weighted, -1, keepdims=True)


def add_pair(first, second):
    return (first[0] + second[0], first[1] + second[1])


def attention_parts(query, keys, tag_window, lengths, feature_proj, first_pos):
    tok_count = query.shape[1]
    key_count = keys.shape[1]
    query_pos = first_pos + jnp.arange(tok_count, dtype=jnp.int32)
    key_pos = first_pos - SPARSE_BLOCK + jnp.arange(key_count, dtype=jnp.int32)
    query_ok = query_pos[None, :] < lengths[:, None]
    key_ok = (key_pos[None, :] >= 0) & (key_pos[None, :] < lengths[:, None])
    own_flag = jnp.arange(key_count) >= SPARSE_BLOCK
    causal = key_pos[None, :] <= query_pos[:, None]
    near_block = key_pos[None, :] // SPARSE_BLOCK >= query_pos[:, None] // SPARSE_BLOCK - 1
    allowed = causal[None, None] & key_ok[:, None, None, :]
    matched = (
        (tag_window[:, :, SPARSE_BLOCK:, None] == tag_window[:, :, None, :])
        & allowed
        & near_block[None, None]
    )
    phi_query = feature_map(query.astype(FLOAT), feature_proj)
    phi_keys = feature_map(keys.astype(FLOAT), feature_proj)
    query_features = phi_query.astype(HALF)
    feat_keys = phi_keys.astype(HALF)
    scores = jnp.einsum(
        "rthd,rjhd->rhtj", query, keys, preferred_element_type=FLOAT
    ) * feature_proj.shape[0] ** (-0.5)
    exponent = jnp.exp(scores)
    approx = jnp.einsum("rthm,rjhm->rhtj", query_features, feat_keys, preferred_element_type=FLOAT)
    blended = jnp.where(
        matched,
        jnp.where(own_flag, exponent, exponent - approx),
        jnp.where(own_flag & allowed, approx, 0.0),
    )
    return (
        query_ok,
        key_ok,
        own_flag,
        allowed,
        matched,
        phi_query,
        phi_keys,
        query_features,
        feat_keys,
        exponent,
        blended,
    )


def per_device(
    tokens,
    lengths,
    buckets,
    feature_proj,
    attn_gain,
    qkv_weight,
    out_weight,
    mlp_gain,
    up_weight,
    down_weight,
    cotangent,
):
    row_count, tok_count, model_width = tokens.shape
    head_count = buckets.shape[1]
    head_size = model_width // head_count
    resid = tokens.astype(FLOAT)
    normed_in = layer_norm(resid, attn_gain).astype(HALF)
    projected = jnp.dot(normed_in, qkv_weight, preferred_element_type=FLOAT).astype(HALF)
    shaped = projected.reshape(row_count, tok_count, 3, head_count, head_size)
    query = shaped[:, :, 0]
    own_keys = shaped[:, :, 1]
    own_values = shaped[:, :, 2]
    tags = buckets.astype(HALF)
    edge_keys, edge_values, edge_tags = from_behind(
        (own_keys[:, -SPARSE_BLOCK:], own_values[:, -SPARSE_BLOCK:], tags[:, :, -SPARSE_BLOCK:]),
        "seq",
        1,
    )
    keys = jnp.concatenate([edge_keys, own_keys], 1)
    value_rows = jnp.concatenate([edge_values, own_values], 1)
    tag_window = jnp.concatenate([edge_tags, tags], 2)
    first_pos = lax.axis_index("seq") * tok_count
    (
        query_ok,
        key_ok,
        own_flag,
        allowed,
        matched,
        phi_query,
        phi_keys,
        query_features,
        feat_keys,
        exponent,
        blended,
    ) = attention_parts(query, keys, tag_window, lengths, feature_proj, first_pos)
    retained_features = jnp.where(
        key_ok[:, SPARSE_BLOCK:, None, None],
        feat_keys[:, SPARSE_BLOCK:],
        jnp.zeros_like(feat_keys[:, SPARSE_BLOCK:]),
    )
    sum_add = jnp.einsum(
        "rthm,rthd->rhmd", retained_features, own_values, preferred_element_type=FLOAT
    )
    norm_add = jnp.sum(retained_features.astype(FLOAT), 1)
    zero_sums = jnp.zeros_like(sum_add)
    zero_norms = jnp.zeros_like(norm_add)
    running_feature_sums, carry_norms = prefix(
        (sum_add, norm_add), "seq", add_pair, (zero_sums, zero_norms), False
    )
    feat_query_f = query_features.astype(FLOAT)
    blended_low = blended.astype(HALF)
    attention_numerator = jnp.einsum(
        "rthm,rhmd->rthd", feat_query_f, running_feature_sums, precision=HIGH_PRECISION
    )
    attention_numerator = attention_numerator + jnp.einsum(
        "rhtj,rjhd->rthd", blended_low, value_rows, preferred_element_type=FLOAT
    )
    denominator = jnp.einsum(
        "rthm,rhm->rth", feat_query_f, carry_norms, precision=HIGH_PRECISION
    ) + jnp.sum(blended, -1).transpose(0, 2, 1)
    den_safe = jnp.where(query_ok[..., None], denominator, 1.0)
    attended = jnp.where(query_ok[..., None, None], attention_numerator / den_safe[..., None], 0.0)
    attended_low = attended.reshape(row_count, tok_count, model_width).astype(HALF)
    mid_resid = resid + jnp.dot(attended_low, out_weight, preferred_element_type=FLOAT)
    normed_mid = layer_norm(mid_resid, mlp_gain).astype(HALF)
    pre_act = jnp.dot(normed_mid, up_weight, preferred_element_type=FLOAT)
    hidden = jax.nn.gelu(pre_act, approximate=True).astype(HALF)
    layer_out = (mid_resid + jnp.dot(hidden, down_weight, preferred_element_type=FLOAT)).astype(
        HALF
    )
    upstream = cotangent.astype(FLOAT)
    grad_down = jnp.einsum("rtf,rtd->fd", hidden, cotangent, preferred_element_type=FLOAT)
    grad_hidden = jnp.einsum("rtd,fd->rtf", cotangent, down_weight, preferred_element_type=FLOAT)
    gelu_vals, gelu_pull = jax.vjp(lambda inner: jax.nn.gelu(inner, approximate=True), pre_act)
    grad_pre = gelu_pull(grad_hidden)[0].astype(HALF)
    grad_up = jnp.einsum("rtd,rtf->df", normed_mid, grad_pre, preferred_element_type=FLOAT)
    grad_normed_mid = jnp.einsum("rtf,df->rtd", grad_pre, up_weight, preferred_element_type=FLOAT)
    mid_vals, mid_pull = jax.vjp(layer_norm, mid_resid, mlp_gain)
    grad_mid_part, grad_mlp_gain = mid_pull(grad_normed_mid)
    grad_mid = upstream + grad_mid_part
    grad_out = jnp.einsum(
        "rtd,rte->de", attended_low.astype(FLOAT), grad_mid, precision=HIGH_PRECISION
    )
    grad_att = jnp.einsum(
        "rte,de->rtd", grad_mid, out_weight.astype(FLOAT), precision=HIGH_PRECISION
    ).astype(HALF)
    grad_att = grad_att.astype(FLOAT).reshape(row_count, tok_count, head_count, head_size)
    grad_numer = jnp.where(query_ok[..., None, None], grad_att / den_safe[..., None], 0.0)
    grad_denom = -jnp.sum(grad_numer * attention_numerator, -1) / den_safe
    grad_feat_query = (
        jnp.einsum("rthd,rhmd->rthm", grad_numer, running_feature_sums, precision=HIGH_PRECISION)
        + grad_denom[..., None] * carry_norms[:, None]
    )
    grad_carry_sums = jnp.einsum(
        "rthm,rthd->rhmd", feat_query_f, grad_numer, precision=HIGH_PRECISION
    )
    grad_carry_norms = jnp.einsum(
        "rthm,rth->rhm", feat_query_f, grad_denom, precision=HIGH_PRECISION
    )
    later_sums, later_norms = prefix(
        (grad_carry_sums, grad_carry_norms), "seq", add_pair, (zero_sums, zero_norms), True
    )
    grad_blend = (
        jnp.einsum(
            "rthd,rjhd->rhtj", grad_numer, value_rows.astype(FLOAT), precision=HIGH_PRECISION
        )
        + grad_denom.transpose(0, 2, 1)[..., None]
    )
    grad_values = jnp.einsum(
        "rhtj,rthd->rjhd", blended_low.astype(FLOAT), grad_numer, precision=HIGH_PRECISION
    )
    grad_expo = jnp.where(matched, grad_blend, 0.0)
    grad_approx = jnp.where(
        matched,
        jnp.where(own_flag, 0.0, -grad_blend),
        jnp.where(own_flag & allowed, grad_blend, 0.0),
    )
    grad_scores = grad_expo * exponent * head_size ** (-0.5)
    grad_query = jnp.einsum(
        "rhtj,rjhd->rthd", grad_scores, keys.astype(FLOAT), precision=HIGH_PRECISION
    )
    grad_keys = jnp.einsum(
        "rhtj,rthd->rjhd", grad_scores, query.astype(FLOAT), precision=HIGH_PRECISION
    )
    grad_feat_query = grad_feat_query + jnp.einsum(
        "rhtj,rjhm->rthm", grad_approx, feat_keys.astype(FLOAT), precision=HIGH_PRECISION
    )
    grad_feat_keys = jnp.einsum(
        "rhtj,rthm->rjhm", grad_approx, feat_query_f, precision=HIGH_PRECISION
    )
    own_mask = key_ok[:, SPARSE_BLOCK:, None, None]
    carry_feat = (
        jnp.einsum(
            "rthd,rhmd->rthm", own_values.astype(FLOAT), later_sums, precision=HIGH_PRECISION
        )
        + later_norms[:, None]
    )
    carry_vals = jnp.einsum(
        "rthm,rhmd->rthd",
        feat_keys[:, SPARSE_BLOCK:].astype(FLOAT),
        later_sums,
        precision=HIGH_PRECISION,
    )
    grad_feat_keys = jnp.concatenate(
        [
            grad_feat_keys[:, :SPARSE_BLOCK],
            grad_feat_keys[:, SPARSE_BLOCK:] + jnp.where(own_mask, carry_feat, 0.0),
        ],
        1,
    )
    grad_values = jnp.concatenate(
        [
            grad_values[:, :SPARSE_BLOCK],
            grad_values[:, SPARSE_BLOCK:] + jnp.where(own_mask, carry_vals, 0.0),
        ],
        1,
    )
    grad_query = grad_query + feature_back(
        query.astype(FLOAT), phi_query, grad_feat_query, feature_proj
    )
    grad_keys = grad_keys + feature_back(keys.astype(FLOAT), phi_keys, grad_feat_keys, feature_proj)
    back_keys, back_values = from_behind(
        (shortened(grad_keys[:, :SPARSE_BLOCK]), shortened(grad_values[:, :SPARSE_BLOCK])),
        "seq",
        -1,
    )
    own_grad_keys = grad_keys[:, SPARSE_BLOCK:]
    own_grad_values = grad_values[:, SPARSE_BLOCK:]
    own_grad_keys = jnp.concatenate(
        [
            own_grad_keys[:, : tok_count - SPARSE_BLOCK],
            own_grad_keys[:, tok_count - SPARSE_BLOCK :] + back_keys,
        ],
        1,
    )
    own_grad_values = jnp.concatenate(
        [
            own_grad_values[:, : tok_count - SPARSE_BLOCK],
            own_grad_values[:, tok_count - SPARSE_BLOCK :] + back_values,
        ],
        1,
    )
    grad_proj = (
        jnp.stack([grad_query, own_grad_keys, own_grad_values], 2)
        .reshape(row_count, tok_count, 3 * model_width)
        .astype(HALF)
    )
    grad_qkv = jnp.einsum("rtd,rte->de", normed_in, grad_proj, preferred_element_type=FLOAT)
    grad_normed_in = jnp.einsum("rte,de->rtd", grad_proj, qkv_weight, preferred_element_type=FLOAT)
    in_vals, in_pull = jax.vjp(layer_norm, resid, attn_gain)
    grad_in_part, grad_attn_gain = in_pull(grad_normed_in)
    grad_tokens = grad_mid + grad_in_part
    shares = (
        lax.psum_scatter(grad_qkv, "seq", scatter_dimension=0, tiled=True),
        lax.psum_scatter(grad_out, "seq", scatter_dimension=0, tiled=True),
        lax.psum_scatter(grad_up, "seq", scatter_dimension=0, tiled=True),
        lax.psum_scatter(grad_down, "seq", scatter_dimension=0, tiled=True),
        lax.psum_scatter(grad_attn_gain, "seq", scatter_dimension=0, tiled=True),
        lax.psum_scatter(grad_mlp_gain, "seq", scatter_dimension=0, tiled=True),
    )
    totals = lax.psum((shares[0], shares[1], shares[2], shares[3], shares[4], shares[5]), "dp")
    return (
        layer_out,
        grad_tokens,
        totals[0],
        totals[1],
        totals[2],
        totals[3],
        totals[4],
        totals[5],
    )


def solution(mesh):
    in_specs = (
        P("dp", "seq", None),
        P("dp"),
        P("dp", None, "seq"),
        P(),
        P(),
        P(),
        P(),
        P(),
        P(),
        P(),
        P("dp", "seq", None),
    )
    out_specs = (
        P("dp", "seq", None),
        P("dp", "seq", None),
        P("seq", None),
        P("seq", None),
        P("seq", None),
        P("seq", None),
        P("seq"),
        P("seq"),
    )
    shape = dict(mesh.shape)
    fast = shape == {"dp": 4, "seq": 8}
    return jax.shard_map(
        per_device_fast if fast else per_device, mesh=mesh, in_specs=in_specs, out_specs=out_specs, check_vma=False
    )
```
